32 devices in a mesh: tm: 16 (over z, y, core), space: 2 (over x).
Axes of the slice: x: 2, y: 2, z: 4, core: 2. Of those that a mesh axis runs over, the one named last changes fastest.
Arguments:
- cpoint_guess: float32 [16, 3, 32, 1024], P('tm', None, 'space'), may hold values from -6 to 6
- tide_forcing: float32 [128, 3, 32, 1024], P('tm', None, 'space'), may hold values from -4 to 4
- depth: float32 [32, 1024], P('space'), may hold values from 0.5 to 1.5
- drag: float32 [32, 1024], P('space'), may hold values from 0.01 to 0.08
Outputs:
- improved: float32 [128, 3, 32, 1024], P('tm', None, 'space')
- cpoint_residual: float32 [16, 3, 32, 1024], P('tm', None, 'space')
The draws below stay inside these ranges and needn't reach their ends.
All inputs are finite; a program needn't handle non-finite values.
Results may differ from the reference program's by a relative error of at most 0.0003.
Values sent between devices are 32-bit elements; how exact they have to be, the bound alone decides.
A program may use at most 128 MiB of HBM per device.

```python
import math
import jax
import jax.numpy as jnp

NY = 1024
T_DEV = 8
LEVELS = 5
NX = 32
TIMES = 128
N_TM = 16


def block_scale(key, extent, split, low, high):
    gain = 1.0
    for position, parts in split:
        draws = jax.random.uniform(jax.random.fold_in(jax.random.fold_in(key, 6), position), (parts,), jnp.float32, low / len(split), high / len(split))
        gain = gain * jnp.repeat(jnp.exp(draws), extent[position] // parts).reshape((-1,) + (1,) * (len(extent) - 1 - position))
    return gain


def centred(key, shape, spread, most, split=(), held_as=jnp.bfloat16):
    gain = block_scale(key, shape, split, -0.22, 0.18) if split else 1.0
    entries = jax.random.normal(key, shape, jnp.float32) * spread * gain
    return jnp.minimum(jnp.maximum(entries, -most), most).astype(held_as)


def setup_inputs(seed: int = 0) -> dict:
    key_list = jax.random.split(jax.random.key(seed), 5)
    cpoint_guess = centred(key_list[0], (N_TM, 3, NX, NY), 1.0, 6.0, ((0, 16), (2, 2)), jnp.float32)
    tide_forcing = centred(key_list[1], (TIMES, 3, NX, NY), 0.5, 4.0, ((0, 16), (2, 2)), jnp.float32)
    depth = jnp.clip(0.5 + 1.0 * jax.random.uniform(key_list[2], (NX, NY), jnp.float32) ** block_scale(key_list[2], (NX, NY), ((0, 2),), -0.2, 0.2), 0.5, 1.5)
    drag = jnp.clip(jnp.exp(math.log(0.08) - 2.0794415 * jax.random.uniform(key_list[3], (NX, NY), jnp.float32) ** block_scale(key_list[3], (NX, NY), ((0, 2),), -0.2, 0.2)), 0.01, 0.08)
    return {"cpoint_guess": cpoint_guess, "tide_forcing": tide_forcing, "depth": depth, "drag": drag}


coriolis = 0.1
fine_courant = 0.25
coarse_courant = 0.5


def along_rows(field):
    return (jnp.roll(field, -1, -2) - jnp.roll(field, 1, -2)) * 0.5


def along_cols(field):
    return (jnp.roll(field, -1, -1) - jnp.roll(field, 1, -1)) * 0.5


def substep(state, depth, drag, courant):
    height = state[..., 0, :, :]
    eastward = state[..., 1, :, :]
    northward = state[..., 2, :, :]
    new_height = height - courant * depth * (along_rows(eastward) + along_cols(northward))
    retain = 1.0 - drag
    new_east = retain * eastward + courant * coriolis * northward - courant * along_rows(new_height)
    new_north = retain * northward - courant * coriolis * eastward - courant * along_cols(new_height)
    return jnp.stack((new_height, new_east, new_north), axis=-3)


def reference(cpoint_guess, tide_forcing, depth, drag):
    forcing = tide_forcing.reshape(N_TM, T_DEV, 3, NX, NY)

    def fine(state):
        return substep(substep(state, depth, drag, fine_courant), depth, drag, fine_courant)

    def coarse(state):
        return substep(state, depth, drag, coarse_courant)

    state = cpoint_guess
    for moment in range(1, T_DEV):
        state = fine(state) + forcing[:, moment]
    right = jnp.roll(fine(state), 1, axis=0) + forcing[:, 0] - cpoint_guess
    rights = [right]
    for level in range(1, LEVELS):
        current = rights[-1]
        earlier = jnp.roll(current, 1, axis=0)[0::2]
        rights.append(current[0::2] + coarse(earlier))
    base = rights[-1]
    points = base.shape[0]
    correction = base
    for counter in range(1, points + 1):
        spot = counter % points
        correction = correction.at[spot].set(coarse(correction[(spot - 1) % points]) + base[spot])
    for level in range(LEVELS - 1, 0, -1):
        current = rights[level - 1]
        odd_points = coarse(correction) + current[1::2]
        correction = jnp.stack((correction, odd_points), axis=1).reshape(current.shape)
    state = cpoint_guess + correction
    states = [state]
    for moment in range(1, T_DEV):
        state = fine(state) + forcing[:, moment]
        states.append(state)
    improved = jnp.stack(states, axis=1).reshape(N_TM * T_DEV, 3, NX, NY)
    return improved, right
```

```python
import jax
import jax.numpy as jnp
from jax import lax
from jax.experimental import pallas as pl
from jax.experimental.pallas import tpu as pltpu
from jax.sharding import PartitionSpec as P

LEVELS = 5


coriolis = 0.1
fine_courant = 0.25
coarse_courant = 0.5


def with_halo(cells, sides, width):
    for axis, dim in sides:
        count = lax.axis_size(axis)
        head = lax.slice_in_dim(cells, 0, width, axis=dim)
        tail = lax.slice_in_dim(cells, cells.shape[dim] - width, cells.shape[dim], axis=dim)
        cells = jnp.concatenate(
            [
                lax.ppermute(tail, axis, [(i, (i + 1) % count) for i in range(count)]),
                cells,
                lax.ppermute(head, axis, [((i + 1) % count, i) for i in range(count)]),
            ],
            axis=dim,
        )
    return cells


def shifted(block, axis, distance):
    devices = range(lax.axis_size(axis))
    route = [((i - distance) % len(devices), i) for i in devices]
    return lax.ppermute(block, axis, route)


def across_rows(field):
    return (field[2:] - field[:-2]) * 0.5


def along_cols(field):
    return (jnp.roll(field, -1, -1) - jnp.roll(field, 1, -1)) * 0.5


def advance(padded, coefficients, courant):
    height = padded[0]
    eastward = padded[1]
    northward = padded[2]
    new_height = height[1:-1] - courant * coefficients[0, 1:-1] * (
        across_rows(eastward) + along_cols(northward)[1:-1]
    )
    retain = 1.0 - coefficients[1, 2:-2]
    east_middle = eastward[2:-2]
    north_middle = northward[2:-2]
    new_east = (
        retain * east_middle + courant * coriolis * north_middle - courant * across_rows(new_height)
    )
    new_north = (
        retain * north_middle
        - courant * coriolis * east_middle
        - courant * along_cols(new_height)[1:-1]
    )
    return jnp.stack((new_height[1:-1], new_east, new_north))


def body(cpoint_guess, tide_forcing, depth, drag):
    coefficients = with_halo(jnp.stack((depth, drag)), (("space", 1),), 4)
    narrow = coefficients[:, 2:-2]

    def one_substep(state, courant):
        padded = with_halo(state, (("space", 1),), 2)
        return advance(padded, narrow, courant)

    def fine_map(state):
        padded = with_halo(state, (("space", 1),), 4)
        middle = advance(padded, coefficients, fine_courant)
        result = advance(middle, narrow, fine_courant)
        return result

    def coarse_map(state):
        return one_substep(state, coarse_courant)

    def pass_on(state, stride, mapper):
        result = shifted(mapper(state), "tm", stride)
        return result

    start = cpoint_guess[0]
    state = start
    for moment in range(1, tide_forcing.shape[0]):
        state = fine_map(state) + tide_forcing[moment]
    right = pass_on(state, 1, fine_map) + tide_forcing[0] - start
    rights = [right]
    for level in range(1, LEVELS):
        current = rights[-1]
        rights.append(current + pass_on(current, 2 ** (level - 1), coarse_map))
    top_stride = 2 ** (LEVELS - 1)
    points = lax.axis_size("tm") // top_stride
    position = lax.axis_index("tm")
    base = rights[-1]
    anchor = position % top_stride == 0

    def sweep(counter, correction):
        arrived = pass_on(correction, top_stride, coarse_map)
        target = jnp.logical_and(anchor, position // top_stride == counter % points)
        return jnp.where(target, arrived + base, correction)

    correction = lax.fori_loop(1, points + 1, sweep, base)
    for level in range(LEVELS - 1, 0, -1):
        stride = 2 ** (level - 1)
        arrived = pass_on(correction, stride, coarse_map)
        odd_point = position % (2 * stride) == stride
        correction = jnp.where(odd_point, arrived + rights[level - 1], correction)
    state = start + correction
    states = [state]
    for moment in range(1, tide_forcing.shape[0]):
        state = fine_map(state) + tide_forcing[moment]
        states.append(state)
    return (jnp.stack(states), right[None])


lanes = 128
group = 4
height_scale = 0.125
early_edges = 3


def cycle_kernel(
    guess_hbm, forcing_hbm, depth_hbm, drag_hbm, out, residual,
    guess, forcing, raw, raw_in, fine_depth, coarse_depth, retain, track, mid, edges, edges_in,
    ahead, ahead_in, first, lift, lift_in, part, part_in, second, third, fourth, climb, wave,
    lower_in, lower, lower_here, own_in, passed, passed_in, relax, relax_mid,
    load_sems, coef_sems, ahead_sems, edge_send, edge_recv, lift_sems, part_send, part_recv,
    second_send, second_recv, third_send, third_recv, fourth_send, fourth_recv, relay_send,
    lower_send, lower_recv, here_sems, own_sems, passed_sems, wave_send, wave_recv, out_sems, go_sem,
):
    tm = lax.axis_index("tm")
    sp = lax.axis_index("space")
    count = lax.axis_size("tm")
    moments = forcing.shape[0]
    own = guess.shape[1]
    rows = 2 * own
    strips = guess.shape[2]
    chunks = rows // group
    other = 1 - sp
    odd = tm % 2
    chip = (tm // 2) % 2
    layer = tm // 4
    pair = layer % 2
    half = layer // 2
    before = (tm + count - 1) % count
    after_chip = (tm + 2) % count
    sibling = tm + 1 - 2 * odd
    facing = tm + 2 - 4 * chip
    beside = tm + 4 - 8 * pair
    inner = pair != half
    inward = (tm + 4 - 8 * half + count) % count

    def load(src, dst, index):
        return [
            pltpu.make_async_copy(
                src.at[..., pl.ds(strip * lanes, lanes)], dst.at[..., strip, :],
                load_sems.at[index, strip],
            )
            for strip in range(strips)
        ]

    loads = [
        load(depth_hbm, raw.at[0], 0),
        load(drag_hbm, raw.at[1], 1),
        load(guess_hbm.at[0], guess, 2),
        load(forcing_hbm.at[0], forcing.at[0], 3),
        load(forcing_hbm.at[1:moments], forcing.at[1:moments], 4),
    ]

    def remote(src, dst, send, recv, to):
        return pltpu.make_async_remote_copy(
            src_ref=src, dst_ref=dst, send_sem=send, recv_sem=recv,
            device_id=to, device_id_type=pl.DeviceIdType.MESH,
        )

    barrier = pltpu.get_barrier_semaphore()
    partners = [(tm, other)]
    for distance in (1, 2, 4):
        partners.append(((tm + distance) % count, sp))
        partners.append(((tm + count - distance) % count, sp))
    for to in partners:
        pl.semaphore_signal(barrier, inc=1, device_id=to, device_id_type=pl.DeviceIdType.MESH)
    for copies in loads:
        for copy in copies:
            copy.start()

    lane = lax.broadcasted_iota(jnp.int32, (1, strips, lanes), 2)

    def down_cols(a):
        here = lax.broadcasted_iota(jnp.int32, a.shape, 2)
        following = jnp.where(here == 0, pltpu.roll(a, strips - 1, 1), a)
        preceding = jnp.where(here == lanes - 1, pltpu.roll(a, 1, 1), a)
        return pltpu.roll(following, lanes - 1, 2) - pltpu.roll(preceding, 1, 2)

    def take(ref, start, size):
        total = ref.shape[0]
        start %= total
        if start + size <= total:
            return ref[start : start + size]
        return jnp.concatenate([ref[start:total], ref[0 : start + size - total]], axis=0)

    def raise_heights(h, u_before, u_after, v, depths):
        return h - depths * (u_after - u_before + down_cols(v))

    def new_speeds(u, v, h_before, h, h_after, kept, courant):
        turn = courant * coriolis
        east = h_after - h_before
        north = down_cols(h)
        slope = courant * 0.5 / height_scale
        if slope != 1.0:
            east = slope * east
            north = slope * north
        return kept * u + turn * v - east, kept * v - turn * u - north

    def fine_substep(src, dst):
        for r in range(0, rows, group):
            dst[0, r : r + group] = raise_heights(
                src[0, r : r + group], take(src.at[1], r - 1, group), take(src.at[1], r + 1, group),
                src[2, r : r + group], fine_depth[r : r + group],
            )
        for r in range(0, rows, group):
            east, north = new_speeds(
                src[1, r : r + group], src[2, r : r + group], take(dst.at[0], r - 1, group),
                dst[0, r : r + group], take(dst.at[0], r + 1, group), retain[r : r + group],
                fine_courant,
            )
            dst[1, r : r + group] = east
            dst[2, r : r + group] = north

    def fine(src, dst):
        fine_substep(src, mid)
        fine_substep(mid, dst)

    def coarse_rows(src, frame, row, size=group):
        start = row - frame
        h = raise_heights(
            take(src.at[0], start - 1, size + 2), take(src.at[1], start - 2, size + 2),
            take(src.at[1], start, size + 2), take(src.at[2], start - 1, size + 2),
            take(coarse_depth, row - 1, size + 2),
        )
        east, north = new_speeds(
            take(src.at[1], start, size), take(src.at[2], start, size), h[0:size],
            h[1 : size + 1], h[2 : size + 2], take(retain, row, size), coarse_courant,
        )
        return h[1 : size + 1], east, north

    def coarse(src, frame, dst, dst_frame, added=None, added_frame=0):
        for r in range(0, rows, group):
            values = coarse_rows(src, frame, r + dst_frame)
            for field in range(3):
                value = values[field]
                if added is not None:
                    value = value + take(added.at[field], r + dst_frame - added_frame, group)
                dst[field, r : r + group] = value

    for copies in loads[:2]:
        for copy in copies:
            copy.wait()
    pl.semaphore_wait(barrier, len(partners))
    coef_copy = remote(raw, raw_in, coef_sems.at[0], coef_sems.at[1], (tm, other))
    coef_copy.start()

    for copies in loads[2:4]:
        for copy in copies:
            copy.wait()

    def scaled(a):
        return jnp.concatenate([a[0:1] * height_scale, a[1:3]], axis=0)

    start_state = scaled(guess[...])
    ahead[...] = scaled(forcing[0]) - start_state
    ahead_copy = remote(ahead, ahead_in, ahead_sems.at[0], ahead_sems.at[1], (before, sp))
    ahead_copy.start()
    guess[...] = start_state
    track[0, :, 0:own] = start_state
    track[0, :, own:rows] = jnp.zeros((3, own, strips, lanes), jnp.float32)
    relax[0] = jnp.zeros((3, own, strips, lanes), jnp.float32)
    fine_depth[0:own] = (fine_courant * 0.5 * height_scale) * raw[0]
    coarse_depth[0:own] = (coarse_courant * 0.5 * height_scale) * raw[0]
    retain[0:own] = 1.0 - raw[1]
    for copy in loads[4]:
        copy.wait()
    coef_copy.wait()
    fine_depth[own:rows] = (fine_courant * 0.5 * height_scale) * raw_in[0]
    coarse_depth[own:rows] = (coarse_courant * 0.5 * height_scale) * raw_in[0]
    retain[own:rows] = 1.0 - raw_in[1]

    def edge_copy(moment):
        return remote(
            edges.at[moment], edges_in.at[moment], edge_send.at[moment], edge_recv.at[moment],
            (tm, other),
        )

    def propagate(moment, carry):
        previous = moment - 1
        src = track.at[previous]
        dst = track.at[moment]
        fine(src, dst)
        for index, (ref, field) in enumerate(((src, 1), (mid, 0), (mid, 1), (dst, 0))):
            edges[previous, 2 * index] = ref[field, 0]
            edges[previous, 2 * index + 1] = ref[field, own - 1]

        @pl.when(previous < early_edges)
        def _():
            edge_copy(previous).start()

        dst[0, 0:own] += height_scale * forcing[moment, 0]
        dst[1, 0:own] += forcing[moment, 1]
        dst[2, 0:own] += forcing[moment, 2]
        return carry

    lax.fori_loop(1, moments, propagate, 0)
    fine(track.at[moments - 1], first)
    ahead_copy.wait()
    first[:, 0:own] += ahead_in[...]

    def bounded(ref, start, size, above, below):
        if start < 0:
            return jnp.concatenate([above[None], ref[0 : start + size]], axis=0)
        if start + size > own:
            return jnp.concatenate([ref[start:own], below[None]], axis=0)
        return ref[start : start + size]

    def relax_substep(src, dst, border, base):
        u_below, u_above = border[base], border[base + 1]
        h_below, h_above = border[base + 2], border[base + 3]
        for r in range(0, own, group):
            dst[0, r : r + group] = raise_heights(
                src[0, r : r + group], bounded(src.at[1], r - 1, group, u_above, u_below),
                bounded(src.at[1], r + 1, group, u_above, u_below), src[2, r : r + group],
                fine_depth[r : r + group],
            )
        for r in range(0, own, group):
            east, north = new_speeds(
                src[1, r : r + group], src[2, r : r + group],
                bounded(dst.at[0], r - 1, group, h_above, h_below), dst[0, r : r + group],
                bounded(dst.at[0], r + 1, group, h_above, h_below), retain[r : r + group],
                fine_courant,
            )
            dst[1, r : r + group] = east
            dst[2, r : r + group] = north

    def relaxed(low, high):
        def step(moment, carry):
            previous = moment - 1
            edge_copy(previous).wait()
            border = edges_in.at[previous]
            a = previous % 2
            b = moment % 2
            relax_substep(relax.at[a], relax_mid, border, 0)
            relax_substep(relax_mid, relax.at[b], border, 4)
            track[moment, :, 0:own] += relax[b]
            return carry

        lax.fori_loop(low, high, step, 0)

    def late_edges():
        def step(moment, carry):
            edge_copy(moment).start()
            return carry

        lax.fori_loop(early_edges, moments - 1, step, 0)

    def span(index):
        return pl.ds(index * group, group)

    lift_copy = remote(lift, lift_in, lift_sems.at[0], lift_sems.at[1], (sibling, sp))
    here_copy = remote(lower, lower_here, here_sems.at[0], here_sems.at[1], (sibling, sp))
    own_copy = remote(
        second.at[chip, :, 0:own], own_in, own_sems.at[0], own_sems.at[1], (sibling, sp)
    )
    passed_copy = remote(passed, passed_in, passed_sems.at[0], passed_sems.at[1], (after_chip, sp))
    lower_copies = [
        remote(
            first.at[:, start : start + own], lower_in.at[:, own - start : rows - start],
            lower_send.at[index], lower_recv.at[1 - index], (tm, other),
        )
        for index, start in enumerate((0, own))
    ]
    top_frame = 4
    wave_copies = [
        remote(
            climb.at[1, :, start:end], wave.at[0, :, (start + top_frame) % rows : (end + top_frame - 1) % rows + 1],
            wave_send.at[index], wave_recv.at[index], (sibling, sp),
        )
        for index, (start, end) in enumerate(((0, own), (own, rows - top_frame), (rows - top_frame, rows)))
    ]

    def part_copy(index):
        landing = (index + chunks // 2) % chunks
        return remote(
            part.at[:, span(index)], part_in.at[:, span(landing)], part_send.at[index],
            part_recv.at[landing], (tm, other),
        )

    def exchange(ref, slot, send, recv, to):
        def copy(index):
            return remote(
                ref.at[slot, :, span(index)], ref.at[slot, :, span(index)], send.at[index],
                recv.at[index], (to, sp),
            )

        return copy

    second_copy = exchange(second, chip, second_send, second_recv, facing)
    second_in = exchange(second, 1 - chip, second_send, second_recv, facing)
    third_copy = exchange(third, pair, third_send, third_recv, beside)
    third_in = exchange(third, 1 - pair, third_send, third_recv, beside)
    fourth_copy = exchange(fourth, half, fourth_send, fourth_recv, inward)
    fourth_in = exchange(fourth, 1 - half, relay_send, fourth_recv, beside)

    @pl.when(odd == 0)
    def _():
        coarse(first, 0, lift, 0)
        lift_copy.start()
        relaxed(1, early_edges + 1)
        pl.semaphore_wait(go_sem, 1)
        late_edges()
        for copy in lower_copies:
            copy.start()
        relaxed(early_edges + 1, moments)
        own_copy.wait_recv()
        for copy in lower_copies:
            copy.wait()
        lower[...] = first[...] + lower_in[...]
        here_copy.start()
        for r in range(0, own, group):
            values = coarse_rows(lower, 0, r)
            for field in range(3):
                passed[field, r : r + group] = own_in[field, r : r + group] - values[field]
        passed_copy.start()
        lift_copy.wait_send()
        passed_copy.wait()
        here_copy.wait_send()
        for copy in wave_copies:
            copy.wait_recv()

    @pl.when(odd == 1)
    def _():
        lift_copy.wait_recv()
        for step in range(chunks):
            index = (step + chunks // 2) % chunks
            here = slice(index * group, (index + 1) * group)
            part[:, here] = first[:, here] + lift_in[:, here]
            part_copy(index).start()
        late_edges()
        relaxed(1, early_edges + 1)

        for index in range(chunks):
            here = slice(index * group, (index + 1) * group)
            part_copy((index + chunks // 2) % chunks).wait_recv()
            second[chip, :, here] = part[:, here] + part_in[:, here]
            second_copy(index).start()
        own_copy.start()
        pl.semaphore_signal(
            go_sem, inc=1, device_id=(sibling, sp), device_id_type=pl.DeviceIdType.MESH
        )

        def ascend(src, arriving, frame, dst, slot, sent, sends):
            for index in range(chunks):
                if index == 0:
                    arriving(0).wait_recv()
                if index + 1 < chunks:
                    arriving(index + 1).wait_recv()
                values = coarse_rows(src.at[0], frame, index * group + frame + 2)
                for field in range(3):
                    dst[slot, field, index * group : (index + 1) * group] = values[field] + take(
                        src.at[1, field], index * group + 2, group
                    )
                if sends is None:
                    sent(index).start()
                else:
                    @pl.when(sends)
                    def _():
                        sent(index).start()

        ascend(second, second_in, 0, third, pair, third_copy, None)
        relaxed(early_edges + 1, moments)
        ascend(third, third_in, 2, fourth, half, fourth_copy, inner)
        for index in range(chunks):
            fourth_in(index).wait_recv()

            @pl.when(inner)
            def _():
                fourth_in(index).start()

        coarse(fourth.at[0], 4, climb.at[0], 4, fourth.at[1], 4)
        coarse(climb.at[0], 4, climb.at[1], 4, climb.at[0], 4)

        def rise(bit, src, dst, added, added_frame):
            @pl.when(bit == 1)
            def _():
                coarse(src, 4, dst, 4, added, added_frame)

            @pl.when(bit == 0)
            def _():
                dst[...] = src[...]

        rise(half, climb.at[1], climb.at[0], fourth.at[0], 4)
        rise(pair, climb.at[0], climb.at[2], third.at[0], 2)
        rise(chip, climb.at[2], climb.at[1], second.at[0], 0)
        for copy in wave_copies:
            copy.start()
        here_copy.wait_recv()
        coarse(climb.at[1], 4, wave.at[0], 0, lower_here, 0)

        own_copy.wait_send()
        for index in range(chunks):
            part_copy(index).wait_send()
            second_copy(index).wait_send()
            third_copy(index).wait_send()

            @pl.when(inner)
            def _():
                fourth_copy(index).wait_send()
                fourth_in(index).wait_send()

        for copy in wave_copies:
            copy.wait_send()

    def store(src, dst, index):
        return [
            pltpu.make_async_copy(
                src.at[:, :, strip, :], dst.at[:, :, pl.ds(strip * lanes, lanes)],
                out_sems.at[index, strip],
            )
            for strip in range(strips)
        ]

    def store_moment(moment):
        return store(track.at[moment, :, 0:own], out.at[moment], moment)

    @pl.when(odd == 1)
    def _():
        own_in[...] = lower_here[:, 0:own]

    @pl.when(odd == 0)
    def _():
        own_in[...] = passed_in[...]

    own_in[0] = own_in[0] * (1.0 / height_scale)
    for copy in store(own_in, residual.at[0], moments):
        copy.start()

    def finish(moment, values):
        track[moment, 0, 0:own] = (1.0 / height_scale) * (values[0] + track[moment, 0, 0:own])
        track[moment, 1, 0:own] += values[1]
        track[moment, 2, 0:own] += values[2]
        for copy in store_moment(moment):
            copy.start()

    finish(0, wave[0, :, 0:own])

    def correct(moment, carry):
        a = (moment - 1) % 2
        b = moment % 2
        fine(wave.at[a], wave.at[b])
        finish(moment, wave[b, :, 0:own])
        return carry

    lax.fori_loop(1, moments, correct, 0)

    def drain(moment, carry):
        for copy in store_moment(moment):
            copy.wait()
        return carry

    lax.fori_loop(0, moments, drain, 0)
    for copy in store(own_in, residual.at[0], moments):
        copy.wait()


def kernel_body(cpoint_guess, tide_forcing, depth, drag):
    moments, fields, own, cols = tide_forcing.shape
    strips = cols // lanes
    rows = 2 * own
    chunks = rows // group

    def held(*shape):
        return pltpu.VMEM((*shape, strips, lanes), jnp.float32)

    dma = pltpu.SemaphoreType.DMA
    vmem = pl.BlockSpec(memory_space=pltpu.VMEM)
    return pl.pallas_call(
        cycle_kernel,
        out_shape=(
            jax.ShapeDtypeStruct(tide_forcing.shape, jnp.float32),
            jax.ShapeDtypeStruct(cpoint_guess.shape, jnp.float32),
        ),
        in_specs=[pl.BlockSpec(memory_space=pltpu.HBM)] * 4,
        out_specs=(vmem, vmem),
        scratch_shapes=[
            held(fields, own),
            held(moments, fields, own),
            held(2, own),
            held(2, own),
            held(rows),
            held(rows),
            held(rows),
            held(moments, fields, rows),
            held(fields, rows),
            held(moments - 1, 8),
            held(moments - 1, 8),
            held(fields, own),
            held(fields, own),
            held(fields, rows),
            held(fields, rows),
            held(fields, rows),
            held(fields, rows),
            held(fields, rows),
            held(2, fields, rows),
            held(2, fields, rows),
            held(2, fields, rows),
            held(3, fields, rows),
            held(2, fields, rows),
            held(fields, rows),
            held(fields, rows),
            held(fields, rows),
            held(fields, own),
            held(fields, own),
            held(fields, own),
            held(2, fields, own),
            held(fields, own),
            dma((5, strips)),
            dma((2,)),
            dma((2,)),
            dma((moments - 1,)),
            dma((moments - 1,)),
            dma((2,)),
            dma((chunks,)),
            dma((chunks,)),
            dma((chunks,)),
            dma((chunks,)),
            dma((chunks,)),
            dma((chunks,)),
            dma((chunks,)),
            dma((chunks,)),
            dma((chunks,)),
            dma((2,)),
            dma((2,)),
            dma((2,)),
            dma((2,)),
            dma((2,)),
            dma((3,)),
            dma((3,)),
            dma((moments + 1, strips)),
            pltpu.SemaphoreType.REGULAR,
        ],
        compiler_params=pltpu.CompilerParams(
            collective_id=0, has_side_effects=True, vmem_limit_bytes=61 * 1024 * 1024
        ),
    )(cpoint_guess, tide_forcing, depth, drag)


def solution(mesh):
    placed = (
        P("tm", None, "space", None),
        P("tm", None, "space", None),
        P("space", None),
        P("space", None),
    )
    one_top_point = mesh.shape["tm"] == 2 ** (LEVELS - 1)
    fits = one_top_point and mesh.shape["space"] == 2
    return jax.shard_map(
        kernel_body if fits else body,
        mesh=mesh,
        in_specs=placed,
        out_specs=(P("tm", None, "space", None), P("tm", None, "space", None)),
        check_vma=False,
    )
```

```python
import jax
import jax.numpy as jnp
from jax import lax
from jax.experimental import pallas as pl
from jax.experimental.pallas import tpu as pltpu
from jax.sharding import PartitionSpec as P

LEVELS = 5


coriolis = 0.1
fine_courant = 0.25
coarse_courant = 0.5


def with_halo(cells, sides, width):
    for axis, dim in sides:
        count = lax.axis_size(axis)
        head = lax.slice_in_dim(cells, 0, width, axis=dim)
        tail = lax.slice_in_dim(cells, cells.shape[dim] - width, cells.shape[dim], axis=dim)
        cells = jnp.concatenate(
            [
                lax.ppermute(tail, axis, [(i, (i + 1) % count) for i in range(count)]),
                cells,
                lax.ppermute(head, axis, [((i + 1) % count, i) for i in range(count)]),
            ],
            axis=dim,
        )
    return cells


def shifted(block, axis, distance):
    devices = range(lax.axis_size(axis))
    route = [((i - distance) % len(devices), i) for i in devices]
    return lax.ppermute(block, axis, route)


def across_rows(field):
    return (field[2:] - field[:-2]) * 0.5


def along_cols(field):
    return (jnp.roll(field, -1, -1) - jnp.roll(field, 1, -1)) * 0.5


def advance(padded, coefficients, courant):
    height = padded[0]
    eastward = padded[1]
    northward = padded[2]
    new_height = height[1:-1] - courant * coefficients[0, 1:-1] * (
        across_rows(eastward) + along_cols(northward)[1:-1]
    )
    retain = 1.0 - coefficients[1, 2:-2]
    east_middle = eastward[2:-2]
    north_middle = northward[2:-2]
    new_east = (
        retain * east_middle + courant * coriolis * north_middle - courant * across_rows(new_height)
    )
    new_north = (
        retain * north_middle
        - courant * coriolis * east_middle
        - courant * along_cols(new_height)[1:-1]
    )
    return jnp.stack((new_height[1:-1], new_east, new_north))


def body(cpoint_guess, tide_forcing, depth, drag):
    coefficients = with_halo(jnp.stack((depth, drag)), (("space", 1),), 4)
    narrow = coefficients[:, 2:-2]

    def one_substep(state, courant):
        padded = with_halo(state, (("space", 1),), 2)
        return advance(padded, narrow, courant)

    def fine_map(state):
        padded = with_halo(state, (("space", 1),), 4)
        middle = advance(padded, coefficients, fine_courant)
        result = advance(middle, narrow, fine_courant)
        return result

    def coarse_map(state):
        return one_substep(state, coarse_courant)

    def pass_on(state, stride, mapper):
        result = shifted(mapper(state), "tm", stride)
        return result

    start = cpoint_guess[0]
    state = start
    for moment in range(1, tide_forcing.shape[0]):
        state = fine_map(state) + tide_forcing[moment]
    right = pass_on(state, 1, fine_map) + tide_forcing[0] - start
    rights = [right]
    for level in range(1, LEVELS):
        current = rights[-1]
        rights.append(current + pass_on(current, 2 ** (level - 1), coarse_map))
    top_stride = 2 ** (LEVELS - 1)
    points = lax.axis_size("tm") // top_stride
    position = lax.axis_index("tm")
    base = rights[-1]
    anchor = position % top_stride == 0

    def sweep(counter, correction):
        arrived = pass_on(correction, top_stride, coarse_map)
        target = jnp.logical_and(anchor, position // top_stride == counter % points)
        return jnp.where(target, arrived + base, correction)

    correction = lax.fori_loop(1, points + 1, sweep, base)
    for level in range(LEVELS - 1, 0, -1):
        stride = 2 ** (level - 1)
        arrived = pass_on(correction, stride, coarse_map)
        odd_point = position % (2 * stride) == stride
        correction = jnp.where(odd_point, arrived + rights[level - 1], correction)
    state = start + correction
    states = [state]
    for moment in range(1, tide_forcing.shape[0]):
        state = fine_map(state) + tide_forcing[moment]
        states.append(state)
    return (jnp.stack(states), right[None])


lanes = 128
group = 4
height_scale = 0.125
early_edges = 3


def down_cols(a):
    here = lax.broadcasted_iota(jnp.int32, a.shape, 2)
    following = jnp.where(here == 0, pltpu.roll(a, a.shape[1] - 1, 1), a)
    preceding = jnp.where(here == lanes - 1, pltpu.roll(a, 1, 1), a)
    return pltpu.roll(following, lanes - 1, 2) - pltpu.roll(preceding, 1, 2)


def take(ref, start, size):
    total = ref.shape[0]
    start %= total
    if start + size <= total:
        return ref[start : start + size]
    return jnp.concatenate([ref[start:total], ref[0 : start + size - total]], axis=0)


def raise_heights(h, u_before, u_after, v, depths):
    return h - depths * (u_after - u_before + down_cols(v))


def new_speeds(u, v, h_before, h, h_after, kept, courant):
    turn = courant * coriolis
    east = h_after - h_before
    north = down_cols(h)
    slope = courant * 0.5 / height_scale
    if slope != 1.0:
        east = slope * east
        north = slope * north
    return kept * u + turn * v - east, kept * v - turn * u - north


def fine_substep(src, dst, depths, kept):
    rows = src.shape[1]
    for r in range(0, rows, group):
        dst[0, r : r + group] = raise_heights(
            src[0, r : r + group], take(src.at[1], r - 1, group), take(src.at[1], r + 1, group),
            src[2, r : r + group], depths[r : r + group],
        )
    for r in range(0, rows, group):
        east, north = new_speeds(
            src[1, r : r + group], src[2, r : r + group], take(dst.at[0], r - 1, group),
            dst[0, r : r + group], take(dst.at[0], r + 1, group), kept[r : r + group],
            fine_courant,
        )
        dst[1, r : r + group] = east
        dst[2, r : r + group] = north


def fine_step(src, middle, dst, depths, kept):
    fine_substep(src, middle, depths, kept)
    fine_substep(middle, dst, depths, kept)


def cycle_kernel(
    guess_hbm, forcing_hbm, depth_hbm, drag_hbm, track, corrected, own_part, fine_depth, retain,
    guess, forcing, raw, raw_in, coarse_depth, mid, edges, edges_in,
    ahead, ahead_in, first, lift, lift_in, part, part_in, second, third, fourth, climb, wave,
    lower_in, lower, lower_here, own_in, passed, passed_in, relax, relax_mid,
    load_sems, coef_sems, ahead_sems, edge_send, edge_recv, lift_sems, part_send, part_recv,
    second_send, second_recv, third_send, third_recv, fourth_send, fourth_recv, relay_send,
    lower_send, lower_recv, here_sems, own_sems, passed_sems, wave_send, wave_recv, go_sem,
):
    tm = lax.axis_index("tm")
    sp = lax.axis_index("space")
    count = lax.axis_size("tm")
    moments = forcing.shape[0]
    own = guess.shape[1]
    rows = 2 * own
    strips = guess.shape[2]
    chunks = rows // group
    other = 1 - sp
    odd = tm % 2
    chip = (tm // 2) % 2
    layer = tm // 4
    pair = layer % 2
    half = layer // 2
    before = (tm + count - 1) % count
    after_chip = (tm + 2) % count
    sibling = tm + 1 - 2 * odd
    facing = tm + 2 - 4 * chip
    beside = tm + 4 - 8 * pair
    inner = pair != half
    inward = (tm + 4 - 8 * half + count) % count

    def load(src, dst, index):
        return [
            pltpu.make_async_copy(
                src.at[..., pl.ds(strip * lanes, lanes)], dst.at[..., strip, :],
                load_sems.at[index, strip],
            )
            for strip in range(strips)
        ]

    loads = [
        load(depth_hbm, raw.at[0], 0),
        load(drag_hbm, raw.at[1], 1),
        load(guess_hbm.at[0], guess, 2),
        load(forcing_hbm.at[0], forcing.at[0], 3),
        load(forcing_hbm.at[1:moments], forcing.at[1:moments], 4),
    ]

    def remote(src, dst, send, recv, to):
        return pltpu.make_async_remote_copy(
            src_ref=src, dst_ref=dst, send_sem=send, recv_sem=recv,
            device_id=to, device_id_type=pl.DeviceIdType.MESH,
        )

    barrier = pltpu.get_barrier_semaphore()
    partners = [(tm, other)]
    for distance in (1, 2, 4):
        partners.append(((tm + distance) % count, sp))
        partners.append(((tm + count - distance) % count, sp))
    for to in partners:
        pl.semaphore_signal(barrier, inc=1, device_id=to, device_id_type=pl.DeviceIdType.MESH)
    for copies in loads:
        for copy in copies:
            copy.start()

    def fine(src, dst):
        fine_step(src, mid, dst, fine_depth, retain)

    def coarse_rows(src, frame, row, size=group):
        start = row - frame
        h = raise_heights(
            take(src.at[0], start - 1, size + 2), take(src.at[1], start - 2, size + 2),
            take(src.at[1], start, size + 2), take(src.at[2], start - 1, size + 2),
            take(coarse_depth, row - 1, size + 2),
        )
        east, north = new_speeds(
            take(src.at[1], start, size), take(src.at[2], start, size), h[0:size],
            h[1 : size + 1], h[2 : size + 2], take(retain, row, size), coarse_courant,
        )
        return h[1 : size + 1], east, north

    def coarse(src, frame, dst, dst_frame, added=None, added_frame=0):
        def plus(value, field, row):
            if added is None:
                return value
            return value + take(added.at[field], row - added_frame, group)

        for r in range(0, rows, group):
            row = r + dst_frame
            start = row - frame
            mid[0, r : r + group] = raise_heights(
                take(src.at[0], start, group), take(src.at[1], start - 1, group),
                take(src.at[1], start + 1, group), take(src.at[2], start, group),
                take(coarse_depth, row, group),
            )
        for r in range(0, rows, group):
            row = r + dst_frame
            start = row - frame
            here = mid[0, r : r + group]
            east, north = new_speeds(
                take(src.at[1], start, group), take(src.at[2], start, group),
                take(mid.at[0], r - 1, group), here, take(mid.at[0], r + 1, group),
                take(retain, row, group), coarse_courant,
            )
            for field, value in enumerate((here, east, north)):
                dst[field, r : r + group] = plus(value, field, row)

    for copies in loads[:2]:
        for copy in copies:
            copy.wait()
    pl.semaphore_wait(barrier, len(partners))
    coef_copy = remote(raw, raw_in, coef_sems.at[0], coef_sems.at[1], (tm, other))
    coef_copy.start()

    for copies in loads[2:4]:
        for copy in copies:
            copy.wait()

    def scaled(a):
        return jnp.concatenate([a[0:1] * height_scale, a[1:3]], axis=0)

    start_state = scaled(guess[...])
    ahead[...] = scaled(forcing[0]) - start_state
    ahead_copy = remote(ahead, ahead_in, ahead_sems.at[0], ahead_sems.at[1], (before, sp))
    ahead_copy.start()
    guess[...] = start_state
    track[0, :, 0:own] = start_state
    track[0, :, own:rows] = jnp.zeros((3, own, strips, lanes), jnp.float32)
    relax[0] = jnp.zeros((3, own, strips, lanes), jnp.float32)
    fine_depth[0:own] = (fine_courant * 0.5 * height_scale) * raw[0]
    coarse_depth[0:own] = (coarse_courant * 0.5 * height_scale) * raw[0]
    retain[0:own] = 1.0 - raw[1]
    for copy in loads[4]:
        copy.wait()
    coef_copy.wait()
    fine_depth[own:rows] = (fine_courant * 0.5 * height_scale) * raw_in[0]
    coarse_depth[own:rows] = (coarse_courant * 0.5 * height_scale) * raw_in[0]
    retain[own:rows] = 1.0 - raw_in[1]

    def edge_copy(moment):
        return remote(
            edges.at[moment], edges_in.at[moment], edge_send.at[moment], edge_recv.at[moment],
            (tm, other),
        )

    def propagate(moment, carry):
        previous = moment - 1
        src = track.at[previous]
        dst = track.at[moment]
        fine(src, dst)
        for index, (ref, field) in enumerate(((src, 1), (mid, 0), (mid, 1), (dst, 0))):
            edges[previous, 2 * index] = ref[field, 0]
            edges[previous, 2 * index + 1] = ref[field, own - 1]

        @pl.when(previous < early_edges)
        def _():
            edge_copy(previous).start()

        dst[0, 0:own] += height_scale * forcing[moment, 0]
        dst[1, 0:own] += forcing[moment, 1]
        dst[2, 0:own] += forcing[moment, 2]
        return carry

    lax.fori_loop(1, moments, propagate, 0)
    fine(track.at[moments - 1], first)
    ahead_copy.wait()
    first[:, 0:own] += ahead_in[...]

    def bounded(ref, start, size, above, below):
        if start < 0:
            return jnp.concatenate([above[None], ref[0 : start + size]], axis=0)
        if start + size > own:
            return jnp.concatenate([ref[start:own], below[None]], axis=0)
        return ref[start : start + size]

    def relax_substep(src, dst, border, base):
        u_below, u_above = border[base], border[base + 1]
        h_below, h_above = border[base + 2], border[base + 3]
        for r in range(0, own, group):
            dst[0, r : r + group] = raise_heights(
                src[0, r : r + group], bounded(src.at[1], r - 1, group, u_above, u_below),
                bounded(src.at[1], r + 1, group, u_above, u_below), src[2, r : r + group],
                fine_depth[r : r + group],
            )
        for r in range(0, own, group):
            east, north = new_speeds(
                src[1, r : r + group], src[2, r : r + group],
                bounded(dst.at[0], r - 1, group, h_above, h_below), dst[0, r : r + group],
                bounded(dst.at[0], r + 1, group, h_above, h_below), retain[r : r + group],
                fine_courant,
            )
            dst[1, r : r + group] = east
            dst[2, r : r + group] = north

    def relaxed(low, high):
        def step(moment, carry):
            previous = moment - 1
            edge_copy(previous).wait()
            border = edges_in.at[previous]
            a = previous % 2
            b = moment % 2
            relax_substep(relax.at[a], relax_mid, border, 0)
            relax_substep(relax_mid, relax.at[b], border, 4)
            track[moment, :, 0:own] += relax[b]
            return carry

        lax.fori_loop(low, high, step, 0)

    def late_edges():
        def step(moment, carry):
            edge_copy(moment).start()
            return carry

        lax.fori_loop(early_edges, moments - 1, step, 0)

    def span(index):
        return pl.ds(index * group, group)

    lift_copy = remote(lift, lift_in, lift_sems.at[0], lift_sems.at[1], (sibling, sp))
    here_copy = remote(lower, lower_here, here_sems.at[0], here_sems.at[1], (sibling, sp))
    own_copy = remote(
        second.at[chip, :, 0:own], own_in, own_sems.at[0], own_sems.at[1], (sibling, sp)
    )
    passed_copy = remote(passed, passed_in, passed_sems.at[0], passed_sems.at[1], (after_chip, sp))
    lower_copies = [
        remote(
            first.at[:, start : start + own], lower_in.at[:, own - start : rows - start],
            lower_send.at[index], lower_recv.at[1 - index], (tm, other),
        )
        for index, start in enumerate((0, own))
    ]
    top_frame = 4
    wave_copies = [
        remote(
            climb.at[1, :, start:end], wave.at[0, :, (start + top_frame) % rows : (end + top_frame - 1) % rows + 1],
            wave_send.at[index], wave_recv.at[index], (sibling, sp),
        )
        for index, (start, end) in enumerate(((0, own), (own, rows - top_frame), (rows - top_frame, rows)))
    ]

    def part_copy(index):
        landing = (index + chunks // 2) % chunks
        return remote(
            part.at[:, span(index)], part_in.at[:, span(landing)], part_send.at[index],
            part_recv.at[landing], (tm, other),
        )

    def exchange(ref, slot, send, recv, to):
        def copy(index):
            return remote(
                ref.at[slot, :, span(index)], ref.at[slot, :, span(index)], send.at[index],
                recv.at[index], (to, sp),
            )

        return copy

    second_copy = exchange(second, chip, second_send, second_recv, facing)
    second_in = exchange(second, 1 - chip, second_send, second_recv, facing)
    third_copy = exchange(third, pair, third_send, third_recv, beside)
    third_in = exchange(third, 1 - pair, third_send, third_recv, beside)
    fourth_copy = exchange(fourth, half, fourth_send, fourth_recv, inward)
    fourth_in = exchange(fourth, 1 - half, relay_send, fourth_recv, beside)

    @pl.when(odd == 0)
    def _():
        coarse(first, 0, lift, 0)
        lift_copy.start()
        relaxed(1, early_edges + 1)
        pl.semaphore_wait(go_sem, 1)
        late_edges()
        for copy in lower_copies:
            copy.start()
        relaxed(early_edges + 1, moments)
        own_copy.wait_recv()
        for copy in lower_copies:
            copy.wait()
        lower[...] = first[...] + lower_in[...]
        here_copy.start()
        for r in range(0, own, group):
            values = coarse_rows(lower, 0, r)
            for field in range(3):
                passed[field, r : r + group] = own_in[field, r : r + group] - values[field]
        passed_copy.start()
        lift_copy.wait_send()
        passed_copy.wait()
        here_copy.wait_send()
        for copy in wave_copies:
            copy.wait_recv()

    @pl.when(odd == 1)
    def _():
        lift_copy.wait_recv()
        for step in range(chunks):
            index = (step + chunks // 2) % chunks
            here = slice(index * group, (index + 1) * group)
            part[:, here] = first[:, here] + lift_in[:, here]
            part_copy(index).start()
        late_edges()
        relaxed(1, early_edges + 1)

        for index in range(chunks):
            here = slice(index * group, (index + 1) * group)
            part_copy((index + chunks // 2) % chunks).wait_recv()
            second[chip, :, here] = part[:, here] + part_in[:, here]
            second_copy(index).start()
        own_copy.start()
        pl.semaphore_signal(
            go_sem, inc=1, device_id=(sibling, sp), device_id_type=pl.DeviceIdType.MESH
        )

        def ascend(src, arriving, frame, dst, slot, sent, sends):
            for index in range(chunks):
                if index == 0:
                    arriving(0).wait_recv()
                if index + 1 < chunks:
                    arriving(index + 1).wait_recv()
                values = coarse_rows(src.at[0], frame, index * group + frame + 2)
                for field in range(3):
                    dst[slot, field, index * group : (index + 1) * group] = values[field] + take(
                        src.at[1, field], index * group + 2, group
                    )
                if sends is None:
                    sent(index).start()
                else:
                    @pl.when(sends)
                    def _():
                        sent(index).start()

        ascend(second, second_in, 0, third, pair, third_copy, None)
        relaxed(early_edges + 1, moments)
        ascend(third, third_in, 2, fourth, half, fourth_copy, inner)
        for index in range(chunks):
            fourth_in(index).wait_recv()

            @pl.when(inner)
            def _():
                fourth_in(index).start()

        coarse(fourth.at[0], 4, climb.at[0], 4, fourth.at[1], 4)
        coarse(climb.at[0], 4, climb.at[1], 4, climb.at[0], 4)

        def rise(bit, src, dst, added, added_frame):
            @pl.when(bit == 1)
            def _():
                coarse(src, 4, dst, 4, added, added_frame)

            @pl.when(bit == 0)
            def _():
                dst[...] = src[...]

        rise(half, climb.at[1], climb.at[0], fourth.at[0], 4)
        rise(pair, climb.at[0], climb.at[2], third.at[0], 2)
        rise(chip, climb.at[2], climb.at[1], second.at[0], 0)
        for copy in wave_copies:
            copy.start()
        here_copy.wait_recv()
        coarse(climb.at[1], 4, wave.at[0], 0, lower_here, 0)

        own_copy.wait_send()
        for index in range(chunks):
            part_copy(index).wait_send()
            second_copy(index).wait_send()
            third_copy(index).wait_send()

            @pl.when(inner)
            def _():
                fourth_copy(index).wait_send()
                fourth_in(index).wait_send()

        for copy in wave_copies:
            copy.wait_send()

    corrected[...] = wave[0]

    @pl.when(odd == 1)
    def _():
        own_part[...] = lower_here[:, 0:own]

    @pl.when(odd == 0)
    def _():
        own_part[...] = passed_in[...]


def finish_kernel(
    track, corrected, own_part, fine_depth, retain, out, residual, wave, mid, ready, ready_part, out_sems
):
    moments, _, own, strips, _ = ready.shape

    def store(src, dst, index):
        return [
            pltpu.make_async_copy(
                src.at[:, :, strip, :], dst.at[:, :, pl.ds(strip * lanes, lanes)],
                out_sems.at[index, strip],
            )
            for strip in range(strips)
        ]

    ready_part[0] = own_part[0] * (1.0 / height_scale)
    ready_part[1:3] = own_part[1:3]
    for copy in store(ready_part, residual.at[0], moments):
        copy.start()

    def finish(moment, values):
        ready[moment, 0] = (1.0 / height_scale) * (values[0] + track[moment, 0, 0:own])
        ready[moment, 1] = values[1] + track[moment, 1, 0:own]
        ready[moment, 2] = values[2] + track[moment, 2, 0:own]
        for copy in store(ready.at[moment], out.at[moment], moment):
            copy.start()

    wave[0] = corrected[...]
    finish(0, corrected[:, 0:own])

    def correct(moment, carry):
        a = (moment - 1) % 2
        b = moment % 2
        fine_step(wave.at[a], mid, wave.at[b], fine_depth, retain)
        finish(moment, wave[b, :, 0:own])
        return carry

    lax.fori_loop(1, moments, correct, 0)

    def drain(moment, carry):
        for copy in store(ready.at[moment], out.at[moment], moment):
            copy.wait()
        return carry

    lax.fori_loop(0, moments, drain, 0)
    for copy in store(ready_part, residual.at[0], moments):
        copy.wait()


def kernel_body(cpoint_guess, tide_forcing, depth, drag):
    moments, fields, own, cols = tide_forcing.shape
    strips = cols // lanes
    rows = 2 * own
    chunks = rows // group

    def held(*shape):
        return pltpu.VMEM((*shape, strips, lanes), jnp.float32)

    dma = pltpu.SemaphoreType.DMA
    vmem = pl.BlockSpec(memory_space=pltpu.VMEM)
    def given(*shape):
        return jax.ShapeDtypeStruct((*shape, strips, lanes), jnp.float32)

    hbm = pl.BlockSpec(memory_space=pltpu.HBM)
    passed_on = pl.pallas_call(
        cycle_kernel,
        out_shape=(
            given(moments, fields, rows),
            given(fields, rows),
            given(fields, own),
            given(rows),
            given(rows),
        ),
        in_specs=[hbm] * 4,
        out_specs=(vmem,) * 5,
        scratch_shapes=[
            held(fields, own),
            held(moments, fields, own),
            held(2, own),
            held(2, own),
            held(rows),
            held(fields, rows),
            held(moments - 1, 8),
            held(moments - 1, 8),
            held(fields, own),
            held(fields, own),
            held(fields, rows),
            held(fields, rows),
            held(fields, rows),
            held(fields, rows),
            held(fields, rows),
            held(2, fields, rows),
            held(2, fields, rows),
            held(2, fields, rows),
            held(3, fields, rows),
            held(2, fields, rows),
            held(fields, rows),
            held(fields, rows),
            held(fields, rows),
            held(fields, own),
            held(fields, own),
            held(fields, own),
            held(2, fields, own),
            held(fields, own),
            dma((5, strips)),
            dma((2,)),
            dma((2,)),
            dma((moments - 1,)),
            dma((moments - 1,)),
            dma((2,)),
            dma((chunks,)),
            dma((chunks,)),
            dma((chunks,)),
            dma((chunks,)),
            dma((chunks,)),
            dma((chunks,)),
            dma((chunks,)),
            dma((chunks,)),
            dma((chunks,)),
            dma((2,)),
            dma((2,)),
            dma((2,)),
            dma((2,)),
            dma((2,)),
            dma((3,)),
            dma((3,)),
            pltpu.SemaphoreType.REGULAR,
        ],
        compiler_params=pltpu.CompilerParams(
            collective_id=0, has_side_effects=True, vmem_limit_bytes=32 * 1024 * 1024
        ),
    )(*(
        pltpu.with_memory_space_constraint(array, pltpu.HBM)
        for array in (cpoint_guess, tide_forcing, depth, drag)
    ))
    return pl.pallas_call(
        finish_kernel,
        out_shape=(
            jax.ShapeDtypeStruct(tide_forcing.shape, jnp.float32),
            jax.ShapeDtypeStruct(cpoint_guess.shape, jnp.float32),
        ),
        in_specs=[vmem] * 5,
        out_specs=(hbm, hbm),
        scratch_shapes=[
            held(2, fields, rows),
            held(fields, rows),
            held(moments, fields, own),
            held(fields, own),
            dma((moments + 1, strips)),
        ],
        compiler_params=pltpu.CompilerParams(vmem_limit_bytes=16 * 1024 * 1024),
    )(*passed_on)


def solution(mesh):
    placed = (
        P("tm", None, "space", None),
        P("tm", None, "space", None),
        P("space", None),
        P("space", None),
    )
    one_top_point = mesh.shape["tm"] == 2 ** (LEVELS - 1)
    fits = one_top_point and mesh.shape["space"] == 2
    return jax.shard_map(
        kernel_body if fits else body,
        mesh=mesh,
        in_specs=placed,
        out_specs=(P("tm", None, "space", None), P("tm", None, "space", None)),
        check_vma=False,
    )
```

```python
import jax
import jax.numpy as jnp
from jax import lax
from jax.experimental import pallas as pl
from jax.experimental.pallas import tpu as pltpu
from jax.sharding import PartitionSpec as P

LEVELS = 5


coriolis = 0.1
fine_courant = 0.25
coarse_courant = 0.5


def with_halo(cells, sides, width):
    for axis, dim in sides:
        count = lax.axis_size(axis)
        head = lax.slice_in_dim(cells, 0, width, axis=dim)
        tail = lax.slice_in_dim(cells, cells.shape[dim] - width, cells.shape[dim], axis=dim)
        cells = jnp.concatenate(
            [
                lax.ppermute(tail, axis, [(i, (i + 1) % count) for i in range(count)]),
                cells,
                lax.ppermute(head, axis, [((i + 1) % count, i) for i in range(count)]),
            ],
            axis=dim,
        )
    return cells


def shifted(block, axis, distance):
    devices = range(lax.axis_size(axis))
    route = [((i - distance) % len(devices), i) for i in devices]
    return lax.ppermute(block, axis, route)


def across_rows(field):
    return (field[2:] - field[:-2]) * 0.5


def along_cols(field):
    return (jnp.roll(field, -1, -1) - jnp.roll(field, 1, -1)) * 0.5


def advance(padded, coefficients, courant):
    height = padded[0]
    eastward = padded[1]
    northward = padded[2]
    new_height = height[1:-1] - courant * coefficients[0, 1:-1] * (
        across_rows(eastward) + along_cols(northward)[1:-1]
    )
    retain = 1.0 - coefficients[1, 2:-2]
    east_middle = eastward[2:-2]
    north_middle = northward[2:-2]
    new_east = (
        retain * east_middle + courant * coriolis * north_middle - courant * across_rows(new_height)
    )
    new_north = (
        retain * north_middle
        - courant * coriolis * east_middle
        - courant * along_cols(new_height)[1:-1]
    )
    return jnp.stack((new_height[1:-1], new_east, new_north))


def body(cpoint_guess, tide_forcing, depth, drag):
    coefficients = with_halo(jnp.stack((depth, drag)), (("space", 1),), 4)
    narrow = coefficients[:, 2:-2]

    def one_substep(state, courant):
        padded = with_halo(state, (("space", 1),), 2)
        return advance(padded, narrow, courant)

    def fine_map(state):
        padded = with_halo(state, (("space", 1),), 4)
        middle = advance(padded, coefficients, fine_courant)
        result = advance(middle, narrow, fine_courant)
        return result

    def coarse_map(state):
        return one_substep(state, coarse_courant)

    def pass_on(state, stride, mapper):
        result = shifted(mapper(state), "tm", stride)
        return result

    start = cpoint_guess[0]
    state = start
    for moment in range(1, tide_forcing.shape[0]):
        state = fine_map(state) + tide_forcing[moment]
    right = pass_on(state, 1, fine_map) + tide_forcing[0] - start
    rights = [right]
    for level in range(1, LEVELS):
        current = rights[-1]
        rights.append(current + pass_on(current, 2 ** (level - 1), coarse_map))
    top_stride = 2 ** (LEVELS - 1)
    points = lax.axis_size("tm") // top_stride
    position = lax.axis_index("tm")
    base = rights[-1]
    anchor = position % top_stride == 0

    def sweep(counter, correction):
        arrived = pass_on(correction, top_stride, coarse_map)
        target = jnp.logical_and(anchor, position // top_stride == counter % points)
        return jnp.where(target, arrived + base, correction)

    correction = lax.fori_loop(1, points + 1, sweep, base)
    for level in range(LEVELS - 1, 0, -1):
        stride = 2 ** (level - 1)
        arrived = pass_on(correction, stride, coarse_map)
        odd_point = position % (2 * stride) == stride
        correction = jnp.where(odd_point, arrived + rights[level - 1], correction)
    state = start + correction
    states = [state]
    for moment in range(1, tide_forcing.shape[0]):
        state = fine_map(state) + tide_forcing[moment]
        states.append(state)
    return (jnp.stack(states), right[None])


lanes = 128
group = 4
piece = 2
lift_piece = 8
height_scale = 0.125
early_edges = 3


def down_cols(a):
    here = lax.broadcasted_iota(jnp.int32, a.shape, 2)
    following = jnp.where(here == 0, pltpu.roll(a, a.shape[1] - 1, 1), a)
    preceding = jnp.where(here == lanes - 1, pltpu.roll(a, 1, 1), a)
    return pltpu.roll(following, lanes - 1, 2) - pltpu.roll(preceding, 1, 2)


def take(ref, start, size):
    total = ref.shape[0]
    start %= total
    if start + size <= total:
        return ref[start : start + size]
    return jnp.concatenate([ref[start:total], ref[0 : start + size - total]], axis=0)


def raise_heights(h, u_before, u_after, v, depths):
    return h - depths * (u_after - u_before + down_cols(v))


def new_speeds(u, v, h_before, h, h_after, kept, courant):
    turn = courant * coriolis
    east = h_after - h_before
    north = down_cols(h)
    slope = courant * 0.5 / height_scale
    if slope != 1.0:
        east = slope * east
        north = slope * north
    return kept * u + turn * v - east, kept * v - turn * u - north


def fine_substep(src, dst, depths, kept):
    rows = src.shape[1]
    for r in range(0, rows, group):
        dst[0, r : r + group] = raise_heights(
            src[0, r : r + group], take(src.at[1], r - 1, group), take(src.at[1], r + 1, group),
            src[2, r : r + group], depths[r : r + group],
        )
    for r in range(0, rows, group):
        east, north = new_speeds(
            src[1, r : r + group], src[2, r : r + group], take(dst.at[0], r - 1, group),
            dst[0, r : r + group], take(dst.at[0], r + 1, group), kept[r : r + group],
            fine_courant,
        )
        dst[1, r : r + group] = east
        dst[2, r : r + group] = north


def fine_step(src, middle, dst, depths, kept):
    fine_substep(src, middle, depths, kept)
    fine_substep(middle, dst, depths, kept)


def cycle_kernel(
    guess_hbm, forcing_hbm, depth_hbm, drag_hbm, track, corrected, own_part, fine_depth, retain,
    guess, forcing, raw, raw_in, coarse_depth, mid, edges, edges_in,
    ahead, ahead_in, first, lift, lift_in, part, part_in, second, third, fourth, climb, wave,
    lower_in, lower, lower_here, own_in, passed, passed_in, relax, relax_mid,
    load_sems, coef_sems, ahead_sems, edge_send, edge_recv, lift_send, lift_recv, part_send, part_recv,
    second_send, second_recv, third_send, third_recv, fourth_send, fourth_recv, relay_send,
    lower_send, lower_recv, here_sems, own_sems, passed_sems, wave_send, wave_recv, go_sem,
):
    tm = lax.axis_index("tm")
    sp = lax.axis_index("space")
    count = lax.axis_size("tm")
    moments = forcing.shape[0]
    own = guess.shape[1]
    rows = 2 * own
    strips = guess.shape[2]
    chunks = rows // piece
    other = 1 - sp
    odd = tm % 2
    chip = (tm // 2) % 2
    layer = tm // 4
    pair = layer % 2
    half = layer // 2
    before = (tm + count - 1) % count
    after_chip = (tm + 2) % count
    sibling = tm + 1 - 2 * odd
    facing = tm + 2 - 4 * chip
    beside = tm + 4 - 8 * pair
    inner = pair != half
    inward = (tm + 4 - 8 * half + count) % count

    def load(src, dst, index):
        return [
            pltpu.make_async_copy(
                src.at[..., pl.ds(strip * lanes, lanes)], dst.at[..., strip, :],
                load_sems.at[index, strip],
            )
            for strip in range(strips)
        ]

    loads = [
        load(depth_hbm, raw.at[0], 0),
        load(drag_hbm, raw.at[1], 1),
        load(guess_hbm.at[0], guess, 2),
        load(forcing_hbm.at[0], forcing.at[0], 3),
        load(forcing_hbm.at[1:moments], forcing.at[1:moments], 4),
    ]

    def remote(src, dst, send, recv, to):
        return pltpu.make_async_remote_copy(
            src_ref=src, dst_ref=dst, send_sem=send, recv_sem=recv,
            device_id=to, device_id_type=pl.DeviceIdType.MESH,
        )

    barrier = pltpu.get_barrier_semaphore()
    partners = [(tm, other)]
    for distance in (1, 2, 4):
        partners.append(((tm + distance) % count, sp))
        partners.append(((tm + count - distance) % count, sp))
    for to in partners:
        pl.semaphore_signal(barrier, inc=1, device_id=to, device_id_type=pl.DeviceIdType.MESH)
    for copies in loads[:2]:
        for copy in copies:
            copy.start()

    def fine(src, dst):
        fine_step(src, mid, dst, fine_depth, retain)

    def coarse_rows(src, frame, row, size=group):
        start = row - frame
        h = raise_heights(
            take(src.at[0], start - 1, size + 2), take(src.at[1], start - 2, size + 2),
            take(src.at[1], start, size + 2), take(src.at[2], start - 1, size + 2),
            take(coarse_depth, row - 1, size + 2),
        )
        east, north = new_speeds(
            take(src.at[1], start, size), take(src.at[2], start, size), h[0:size],
            h[1 : size + 1], h[2 : size + 2], take(retain, row, size), coarse_courant,
        )
        return h[1 : size + 1], east, north

    def coarse(src, frame, dst, dst_frame, added=None, added_frame=0):
        def plus(value, field, row):
            if added is None:
                return value
            return value + take(added.at[field], row - added_frame, group)

        for r in range(0, rows, group):
            row = r + dst_frame
            start = row - frame
            mid[0, r : r + group] = raise_heights(
                take(src.at[0], start, group), take(src.at[1], start - 1, group),
                take(src.at[1], start + 1, group), take(src.at[2], start, group),
                take(coarse_depth, row, group),
            )
        for r in range(0, rows, group):
            row = r + dst_frame
            start = row - frame
            here = mid[0, r : r + group]
            east, north = new_speeds(
                take(src.at[1], start, group), take(src.at[2], start, group),
                take(mid.at[0], r - 1, group), here, take(mid.at[0], r + 1, group),
                take(retain, row, group), coarse_courant,
            )
            for field, value in enumerate((here, east, north)):
                dst[field, r : r + group] = plus(value, field, row)

    for copies in loads[:2]:
        for copy in copies:
            copy.wait()
    pl.semaphore_wait(barrier, len(partners))
    middle = own // 2
    mine = pl.ds(odd * middle, middle)
    theirs = pl.ds((1 - odd) * middle, middle)
    coef_copy = remote(
        raw.at[:, mine], raw_in.at[:, mine], coef_sems.at[0], coef_sems.at[1], (tm, other)
    )
    coef_share = remote(
        raw_in.at[:, mine], raw_in.at[:, mine], coef_sems.at[2], coef_sems.at[3], (sibling, sp)
    )
    coef_shared = remote(
        raw_in.at[:, theirs], raw_in.at[:, theirs], coef_sems.at[2], coef_sems.at[3], (sibling, sp)
    )
    coef_copy.start()
    for copies in loads[2:]:
        for copy in copies:
            copy.start()

    for copies in loads[2:4]:
        for copy in copies:
            copy.wait()

    def scaled(a):
        return jnp.concatenate([a[0:1] * height_scale, a[1:3]], axis=0)

    start_state = scaled(guess[...])
    ahead[...] = scaled(forcing[0]) - start_state
    ahead_copy = remote(ahead, ahead_in, ahead_sems.at[0], ahead_sems.at[1], (before, sp))
    ahead_copy.start()
    guess[...] = start_state
    track[0, :, 0:own] = start_state
    track[0, :, own:rows] = jnp.zeros((3, own, strips, lanes), jnp.float32)
    relax[0] = jnp.zeros((3, own, strips, lanes), jnp.float32)
    fine_depth[0:own] = (fine_courant * 0.5 * height_scale) * raw[0]
    coarse_depth[0:own] = (coarse_courant * 0.5 * height_scale) * raw[0]
    retain[0:own] = 1.0 - raw[1]
    coef_copy.wait_recv()
    coef_share.start()
    for copy in loads[4]:
        copy.wait()
    coef_copy.wait_send()
    coef_shared.wait_recv()
    coef_share.wait_send()
    fine_depth[own:rows] = (fine_courant * 0.5 * height_scale) * raw_in[0]
    coarse_depth[own:rows] = (coarse_courant * 0.5 * height_scale) * raw_in[0]
    retain[own:rows] = 1.0 - raw_in[1]

    def edge_copy(moment):
        return remote(
            edges.at[moment], edges_in.at[moment], edge_send.at[moment], edge_recv.at[moment],
            (tm, other),
        )

    def propagate(moment, carry):
        previous = moment - 1
        src = track.at[previous]
        dst = track.at[moment]
        fine(src, dst)
        for index, (ref, field) in enumerate(((src, 1), (mid, 0), (mid, 1), (dst, 0))):
            edges[previous, 2 * index] = ref[field, 0]
            edges[previous, 2 * index + 1] = ref[field, own - 1]

        @pl.when(previous < early_edges)
        def _():
            edge_copy(previous).start()

        dst[0, 0:own] += height_scale * forcing[moment, 0]
        dst[1, 0:own] += forcing[moment, 1]
        dst[2, 0:own] += forcing[moment, 2]
        return carry

    lax.fori_loop(1, moments, propagate, 0)
    fine(track.at[moments - 1], first)
    ahead_copy.wait()
    first[:, 0:own] += ahead_in[...]

    def bounded(ref, start, size, above, below):
        if start < 0:
            return jnp.concatenate([above[None], ref[0 : start + size]], axis=0)
        if start + size > own:
            return jnp.concatenate([ref[start:own], below[None]], axis=0)
        return ref[start : start + size]

    def relax_substep(src, dst, border, base):
        u_below, u_above = border[base], border[base + 1]
        h_below, h_above = border[base + 2], border[base + 3]
        for r in range(0, own, group):
            dst[0, r : r + group] = raise_heights(
                src[0, r : r + group], bounded(src.at[1], r - 1, group, u_above, u_below),
                bounded(src.at[1], r + 1, group, u_above, u_below), src[2, r : r + group],
                fine_depth[r : r + group],
            )
        for r in range(0, own, group):
            east, north = new_speeds(
                src[1, r : r + group], src[2, r : r + group],
                bounded(dst.at[0], r - 1, group, h_above, h_below), dst[0, r : r + group],
                bounded(dst.at[0], r + 1, group, h_above, h_below), retain[r : r + group],
                fine_courant,
            )
            dst[1, r : r + group] = east
            dst[2, r : r + group] = north

    def relaxed(low, high):
        def step(moment, carry):
            previous = moment - 1
            edge_copy(previous).wait()
            border = edges_in.at[previous]
            a = previous % 2
            b = moment % 2
            relax_substep(relax.at[a], relax_mid, border, 0)
            relax_substep(relax_mid, relax.at[b], border, 4)
            track[moment, :, 0:own] += relax[b]
            return carry

        lax.fori_loop(low, high, step, 0)

    def late_edges():
        def step(moment, carry):
            edge_copy(moment).start()
            return carry

        lax.fori_loop(early_edges, moments - 1, step, 0)

    def span(index):
        return pl.ds(index * piece, piece)

    lift_pieces = rows // lift_piece
    lift_order = [(index + lift_pieces // 2) % lift_pieces for index in range(lift_pieces)]

    def lift_copy(index):
        here = pl.ds(index * lift_piece, lift_piece)
        return remote(
            lift.at[:, here], lift_in.at[:, here], lift_send.at[index], lift_recv.at[index],
            (sibling, sp),
        )

    here_copy = remote(lower, lower_here, here_sems.at[0], here_sems.at[1], (sibling, sp))
    own_copy = remote(
        second.at[chip, :, 0:own], own_in, own_sems.at[0], own_sems.at[1], (sibling, sp)
    )
    passed_copy = remote(passed, passed_in, passed_sems.at[0], passed_sems.at[1], (after_chip, sp))
    lower_copies = [
        remote(
            first.at[:, start : start + own], lower_in.at[:, own - start : rows - start],
            lower_send.at[index], lower_recv.at[1 - index], (tm, other),
        )
        for index, start in enumerate((0, own))
    ]
    top_frame = 4
    wave_pieces = ((0, own), (own, rows - top_frame), (rows - top_frame, rows))
    wave_copies = [
        remote(
            climb.at[1, :, start:end], wave.at[0, :, (start + top_frame) % rows : (end + top_frame - 1) % rows + 1],
            wave_send.at[index], wave_recv.at[index], (sibling, sp),
        )
        for index, (start, end) in enumerate(wave_pieces)
    ]

    def part_copy(index):
        landing = (index + chunks // 2) % chunks
        return remote(
            part.at[:, span(index)], part_in.at[:, span(landing)], part_send.at[index],
            part_recv.at[landing], (tm, other),
        )

    def exchange(ref, slot, send, recv, to):
        def copy(index):
            return remote(
                ref.at[slot, :, span(index)], ref.at[slot, :, span(index)], send.at[index],
                recv.at[index], (to, sp),
            )

        return copy

    second_copy = exchange(second, chip, second_send, second_recv, facing)
    second_in = exchange(second, 1 - chip, second_send, second_recv, facing)
    third_copy = exchange(third, pair, third_send, third_recv, beside)
    third_in = exchange(third, 1 - pair, third_send, third_recv, beside)
    fourth_copy = exchange(fourth, half, fourth_send, fourth_recv, inward)
    fourth_in = exchange(fourth, 1 - half, relay_send, fourth_recv, beside)

    @pl.when(odd == 0)
    def _():
        for index in lift_order:
            start = index * lift_piece
            values = coarse_rows(first, 0, start, lift_piece)
            for field in range(3):
                lift[field, start : start + lift_piece] = values[field]
            lift_copy(index).start()
        relaxed(1, early_edges + 1)
        pl.semaphore_wait(go_sem, 1)
        for copy in lower_copies:
            copy.start()
        late_edges()
        own_copy.wait_recv()
        for copy in lower_copies:
            copy.wait()
        lower[...] = first[...] + lower_in[...]
        here_copy.start()
        for r in range(0, own, group):
            values = coarse_rows(lower, 0, r)
            for field in range(3):
                passed[field, r : r + group] = own_in[field, r : r + group] - values[field]
        passed_copy.start()
        relaxed(early_edges + 1, moments)
        for index in lift_order:
            lift_copy(index).wait_send()
        passed_copy.wait()
        here_copy.wait_send()
        for copy in wave_copies:
            copy.wait_recv()

    @pl.when(odd == 1)
    def _():
        for index in lift_order:
            lift_copy(index).wait_recv()
            for inside in range(lift_piece // piece):
                chunk = index * (lift_piece // piece) + inside
                here = slice(chunk * piece, (chunk + 1) * piece)
                part[:, here] = first[:, here] + lift_in[:, here]
                part_copy(chunk).start()
        late_edges()
        relaxed(1, early_edges + 1)

        for index in range(chunks):
            here = slice(index * piece, (index + 1) * piece)
            part_copy((index + chunks // 2) % chunks).wait_recv()
            second[chip, :, here] = part[:, here] + part_in[:, here]
            second_copy(index).start()
            if index == chunks // 2:
                pl.semaphore_signal(
                    go_sem, inc=1, device_id=(sibling, sp), device_id_type=pl.DeviceIdType.MESH
                )

        own_copy.start()

        def ascend(src, arriving, frame, dst, slot, sent, sends):
            for index in range(chunks):
                if index == 0:
                    arriving(0).wait_recv()
                    arriving(1).wait_recv()
                if index + 2 < chunks:
                    arriving(index + 2).wait_recv()
                values = coarse_rows(src.at[0], frame, index * piece + frame + 2, piece)
                for field in range(3):
                    dst[slot, field, index * piece : (index + 1) * piece] = values[field] + take(
                        src.at[1, field], index * piece + 2, piece
                    )
                if sends is None:
                    sent(index).start()
                else:
                    @pl.when(sends)
                    def _():
                        sent(index).start()

        ascend(second, second_in, 0, third, pair, third_copy, None)
        relaxed(early_edges + 1, moments)
        ascend(third, third_in, 2, fourth, half, fourth_copy, inner)
        for index in range(chunks):
            fourth_in(index).wait_recv()

            @pl.when(inner)
            def _():
                fourth_in(index).start()

        coarse(fourth.at[0], 4, climb.at[0], 4, fourth.at[1], 4)
        coarse(climb.at[0], 4, climb.at[1], 4, climb.at[0], 4)

        def rise(bit, src, dst, added, added_frame):
            @pl.when(bit == 1)
            def _():
                coarse(src, 4, dst, 4, added, added_frame)

            @pl.when(bit == 0)
            def _():
                dst[...] = src[...]

        rise(half, climb.at[1], climb.at[0], fourth.at[0], 4)
        rise(pair, climb.at[0], climb.at[2], third.at[0], 2)

        for (start, end), copy in zip(wave_pieces, wave_copies):
            @pl.when(chip == 1)
            def _():
                values = coarse_rows(climb.at[2], 4, start + 4, end - start)
                for field in range(3):
                    climb[1, field, start:end] = values[field] + take(
                        second.at[0, field], start + 4, end - start
                    )

            @pl.when(chip == 0)
            def _():
                climb[1, :, start:end] = climb[2, :, start:end]

            copy.start()
        here_copy.wait_recv()
        coarse(climb.at[1], 4, wave.at[0], 0, lower_here, 0)

        own_copy.wait_send()
        for index in range(chunks):
            part_copy(index).wait_send()
            second_copy(index).wait_send()
            third_copy(index).wait_send()

            @pl.when(inner)
            def _():
                fourth_copy(index).wait_send()
                fourth_in(index).wait_send()

        for copy in wave_copies:
            copy.wait_send()

    corrected[...] = wave[0]

    @pl.when(odd == 1)
    def _():
        own_part[...] = lower_here[:, 0:own]

    @pl.when(odd == 0)
    def _():
        own_part[...] = passed_in[...]


def finish_kernel(
    track, corrected, own_part, fine_depth, retain, out, residual, wave, mid, ready, ready_part, out_sems
):
    moments, _, own, strips, _ = ready.shape

    def store(src, dst, index):
        return [
            pltpu.make_async_copy(
                src.at[:, :, strip, :], dst.at[:, :, pl.ds(strip * lanes, lanes)],
                out_sems.at[index, strip],
            )
            for strip in range(strips)
        ]

    def ready_copies(moment):
        return store(ready.at[moment], out.at[moment], moment)

    def finish(moment, values):
        ready[moment, 0] = (1.0 / height_scale) * (values[0] + track[moment, 0, 0:own])
        ready[moment, 1] = values[1] + track[moment, 1, 0:own]
        ready[moment, 2] = values[2] + track[moment, 2, 0:own]

    finish(0, corrected[:, 0:own])
    ready_part[0] = own_part[0] * (1.0 / height_scale)
    ready_part[1:3] = own_part[1:3]
    for copy in store(ready_part, residual.at[0], moments):
        copy.start()
    fine_step(corrected, mid, wave.at[1], fine_depth, retain)
    finish(1, wave[1, :, 0:own])
    for copy in ready_copies(0):
        copy.start()

    def correct(moment, carry):
        a = (moment - 1) % 2
        b = moment % 2
        for copy in ready_copies(moment - 1):
            copy.start()
        fine_step(wave.at[a], mid, wave.at[b], fine_depth, retain)
        finish(moment, wave[b, :, 0:own])
        return carry

    lax.fori_loop(2, moments, correct, 0)
    for copy in ready_copies(moments - 1):
        copy.start()

    def drain(moment, carry):
        for copy in ready_copies(moment):
            copy.wait()
        return carry

    lax.fori_loop(0, moments, drain, 0)
    for copy in store(ready_part, residual.at[0], moments):
        copy.wait()


def kernel_body(cpoint_guess, tide_forcing, depth, drag):
    moments, fields, own, cols = tide_forcing.shape
    strips = cols // lanes
    rows = 2 * own
    chunks = rows // piece

    def held(*shape):
        return pltpu.VMEM((*shape, strips, lanes), jnp.float32)

    dma = pltpu.SemaphoreType.DMA
    vmem = pl.BlockSpec(memory_space=pltpu.VMEM)
    def given(*shape):
        return jax.ShapeDtypeStruct((*shape, strips, lanes), jnp.float32)

    hbm = pl.BlockSpec(memory_space=pltpu.HBM)
    passed_on = pl.pallas_call(
        cycle_kernel,
        out_shape=(
            given(moments, fields, rows),
            given(fields, rows),
            given(fields, own),
            given(rows),
            given(rows),
        ),
        in_specs=[hbm] * 4,
        out_specs=(vmem,) * 5,
        scratch_shapes=[
            held(fields, own),
            held(moments, fields, own),
            held(2, own),
            held(2, own),
            held(rows),
            held(fields, rows),
            held(moments - 1, 8),
            held(moments - 1, 8),
            held(fields, own),
            held(fields, own),
            held(fields, rows),
            held(fields, rows),
            held(fields, rows),
            held(fields, rows),
            held(fields, rows),
            held(2, fields, rows),
            held(2, fields, rows),
            held(2, fields, rows),
            held(3, fields, rows),
            held(2, fields, rows),
            held(fields, rows),
            held(fields, rows),
            held(fields, rows),
            held(fields, own),
            held(fields, own),
            held(fields, own),
            held(2, fields, own),
            held(fields, own),
            dma((5, strips)),
            dma((4,)),
            dma((2,)),
            dma((moments - 1,)),
            dma((moments - 1,)),
            dma((rows // lift_piece,)),
            dma((rows // lift_piece,)),
            dma((chunks,)),
            dma((chunks,)),
            dma((chunks,)),
            dma((chunks,)),
            dma((chunks,)),
            dma((chunks,)),
            dma((chunks,)),
            dma((chunks,)),
            dma((chunks,)),
            dma((2,)),
            dma((2,)),
            dma((2,)),
            dma((2,)),
            dma((2,)),
            dma((3,)),
            dma((3,)),
            pltpu.SemaphoreType.REGULAR,
        ],
        compiler_params=pltpu.CompilerParams(
            collective_id=0, has_side_effects=True, vmem_limit_bytes=32 * 1024 * 1024
        ),
    )(*(
        pltpu.with_memory_space_constraint(array, pltpu.HBM)
        for array in (cpoint_guess, tide_forcing, depth, drag)
    ))
    return pl.pallas_call(
        finish_kernel,
        out_shape=(
            jax.ShapeDtypeStruct(tide_forcing.shape, jnp.float32),
            jax.ShapeDtypeStruct(cpoint_guess.shape, jnp.float32),
        ),
        in_specs=[vmem] * 5,
        out_specs=(hbm, hbm),
        scratch_shapes=[
            held(2, fields, rows),
            held(fields, rows),
            held(moments, fields, own),
            held(fields, own),
            dma((moments + 1, strips)),
        ],
        compiler_params=pltpu.CompilerParams(vmem_limit_bytes=16 * 1024 * 1024),
    )(*passed_on)


def solution(mesh):
    placed = (
        P("tm", None, "space", None),
        P("tm", None, "space", None),
        P("space", None),
        P("space", None),
    )
    one_top_point = mesh.shape["tm"] == 2 ** (LEVELS - 1)
    fits = one_top_point and mesh.shape["space"] == 2
    return jax.shard_map(
        kernel_body if fits else body,
        mesh=mesh,
        in_specs=placed,
        out_specs=(P("tm", None, "space", None), P("tm", None, "space", None)),
        check_vma=False,
    )
```

```python
import jax
import jax.numpy as jnp
from jax import lax
from jax.experimental import pallas as pl
from jax.experimental.pallas import tpu as pltpu
from jax.sharding import PartitionSpec as P

LEVELS = 5


coriolis = 0.1
fine_courant = 0.25
coarse_courant = 0.5


def with_halo(cells, sides, width):
    for axis, dim in sides:
        count = lax.axis_size(axis)
        head = lax.slice_in_dim(cells, 0, width, axis=dim)
        tail = lax.slice_in_dim(cells, cells.shape[dim] - width, cells.shape[dim], axis=dim)
        cells = jnp.concatenate(
            [
                lax.ppermute(tail, axis, [(i, (i + 1) % count) for i in range(count)]),
                cells,
                lax.ppermute(head, axis, [((i + 1) % count, i) for i in range(count)]),
            ],
            axis=dim,
        )
    return cells


def shifted(block, axis, distance):
    devices = range(lax.axis_size(axis))
    route = [((i - distance) % len(devices), i) for i in devices]
    return lax.ppermute(block, axis, route)


def across_rows(field):
    return (field[2:] - field[:-2]) * 0.5


def along_cols(field):
    return (jnp.roll(field, -1, -1) - jnp.roll(field, 1, -1)) * 0.5


def advance(padded, coefficients, courant):
    height = padded[0]
    eastward = padded[1]
    northward = padded[2]
    new_height = height[1:-1] - courant * coefficients[0, 1:-1] * (
        across_rows(eastward) + along_cols(northward)[1:-1]
    )
    retain = 1.0 - coefficients[1, 2:-2]
    east_middle = eastward[2:-2]
    north_middle = northward[2:-2]
    new_east = (
        retain * east_middle + courant * coriolis * north_middle - courant * across_rows(new_height)
    )
    new_north = (
        retain * north_middle
        - courant * coriolis * east_middle
        - courant * along_cols(new_height)[1:-1]
    )
    return jnp.stack((new_height[1:-1], new_east, new_north))


def body(cpoint_guess, tide_forcing, depth, drag):
    coefficients = with_halo(jnp.stack((depth, drag)), (("space", 1),), 4)
    narrow = coefficients[:, 2:-2]

    def one_substep(state, courant):
        padded = with_halo(state, (("space", 1),), 2)
        return advance(padded, narrow, courant)

    def fine_map(state):
        padded = with_halo(state, (("space", 1),), 4)
        middle = advance(padded, coefficients, fine_courant)
        result = advance(middle, narrow, fine_courant)
        return result

    def coarse_map(state):
        return one_substep(state, coarse_courant)

    def pass_on(state, stride, mapper):
        result = shifted(mapper(state), "tm", stride)
        return result

    start = cpoint_guess[0]
    state = start
    for moment in range(1, tide_forcing.shape[0]):
        state = fine_map(state) + tide_forcing[moment]
    right = pass_on(state, 1, fine_map) + tide_forcing[0] - start
    rights = [right]
    for level in range(1, LEVELS):
        current = rights[-1]
        rights.append(current + pass_on(current, 2 ** (level - 1), coarse_map))
    top_stride = 2 ** (LEVELS - 1)
    points = lax.axis_size("tm") // top_stride
    position = lax.axis_index("tm")
    base = rights[-1]
    anchor = position % top_stride == 0

    def sweep(counter, correction):
        arrived = pass_on(correction, top_stride, coarse_map)
        target = jnp.logical_and(anchor, position // top_stride == counter % points)
        return jnp.where(target, arrived + base, correction)

    correction = lax.fori_loop(1, points + 1, sweep, base)
    for level in range(LEVELS - 1, 0, -1):
        stride = 2 ** (level - 1)
        arrived = pass_on(correction, stride, coarse_map)
        odd_point = position % (2 * stride) == stride
        correction = jnp.where(odd_point, arrived + rights[level - 1], correction)
    state = start + correction
    states = [state]
    for moment in range(1, tide_forcing.shape[0]):
        state = fine_map(state) + tide_forcing[moment]
        states.append(state)
    return (jnp.stack(states), right[None])


lanes = 128
group = 4
piece = 2
lift_piece = 8
height_scale = 0.125
early_edges = 3


def down_cols(a):
    here = lax.broadcasted_iota(jnp.int32, a.shape, 2)
    following = jnp.where(here == 0, pltpu.roll(a, a.shape[1] - 1, 1), a)
    preceding = jnp.where(here == lanes - 1, pltpu.roll(a, 1, 1), a)
    return pltpu.roll(following, lanes - 1, 2) - pltpu.roll(preceding, 1, 2)


def take(ref, start, size):
    total = ref.shape[0]
    start %= total
    if start + size <= total:
        return ref[start : start + size]
    return jnp.concatenate([ref[start:total], ref[0 : start + size - total]], axis=0)


def raise_heights(h, u_before, u_after, v, depths):
    return h - depths * (u_after - u_before + down_cols(v))


def new_speeds(u, v, h_before, h, h_after, kept, courant):
    turn = courant * coriolis
    east = h_after - h_before
    north = down_cols(h)
    slope = courant * 0.5 / height_scale
    if slope != 1.0:
        east = slope * east
        north = slope * north
    return kept * u + turn * v - east, kept * v - turn * u - north


def fine_substep(src, dst, depths, kept):
    rows = src.shape[1]
    for r in range(0, rows, group):
        dst[0, r : r + group] = raise_heights(
            src[0, r : r + group], take(src.at[1], r - 1, group), take(src.at[1], r + 1, group),
            src[2, r : r + group], depths[r : r + group],
        )
    for r in range(0, rows, group):
        east, north = new_speeds(
            src[1, r : r + group], src[2, r : r + group], take(dst.at[0], r - 1, group),
            dst[0, r : r + group], take(dst.at[0], r + 1, group), kept[r : r + group],
            fine_courant,
        )
        dst[1, r : r + group] = east
        dst[2, r : r + group] = north


def fine_step(src, middle, dst, depths, kept):
    fine_substep(src, middle, depths, kept)
    fine_substep(middle, dst, depths, kept)


def cycle_kernel(
    guess_hbm, forcing_hbm, depth_hbm, drag_hbm, track, corrected, own_part, fine_depth, retain,
    guess, forcing, raw, raw_in, coarse_depth, mid, edges, edges_in,
    ahead, ahead_in, first, lift, lift_in, part, part_in, second, third, fourth, climb, wave,
    lower_in, lower, lower_here, own_in, passed, passed_in, relax, relax_mid,
    load_sems, coef_sems, ahead_sems, edge_send, edge_recv, lift_send, lift_recv, part_send, part_recv,
    second_send, second_recv, third_send, third_recv, fourth_send, fourth_recv, relay_send,
    lower_send, lower_recv, here_sems, own_sems, passed_sems, wave_send, wave_recv, go_sem,
):
    tm = lax.axis_index("tm")
    sp = lax.axis_index("space")
    count = lax.axis_size("tm")
    moments = forcing.shape[0]
    own = guess.shape[1]
    rows = 2 * own
    strips = guess.shape[2]
    chunks = rows // piece
    other = 1 - sp
    odd = tm % 2
    chip = (tm // 2) % 2
    layer = tm // 4
    pair = layer % 2
    half = layer // 2
    before = (tm + count - 1) % count
    after_chip = (tm + 2) % count
    sibling = tm + 1 - 2 * odd
    facing = tm + 2 - 4 * chip
    beside = tm + 4 - 8 * pair
    inner = pair != half
    inward = (tm + 4 - 8 * half + count) % count

    def load(src, dst, index):
        return [
            pltpu.make_async_copy(
                src.at[..., pl.ds(strip * lanes, lanes)], dst.at[..., strip, :],
                load_sems.at[index, strip],
            )
            for strip in range(strips)
        ]

    loads = [
        load(depth_hbm, raw.at[0], 0),
        load(drag_hbm, raw.at[1], 1),
        load(guess_hbm.at[0], guess, 2),
        load(forcing_hbm.at[0], forcing.at[0], 3),
        load(forcing_hbm.at[1:moments], forcing.at[1:moments], 4),
    ]

    def remote(src, dst, send, recv, to):
        return pltpu.make_async_remote_copy(
            src_ref=src, dst_ref=dst, send_sem=send, recv_sem=recv,
            device_id=to, device_id_type=pl.DeviceIdType.MESH,
        )

    barrier = pltpu.get_barrier_semaphore()
    partners = [(tm, other)]
    for distance in (1, 2, 4):
        partners.append(((tm + distance) % count, sp))
        partners.append(((tm + count - distance) % count, sp))
    for to in partners:
        pl.semaphore_signal(barrier, inc=1, device_id=to, device_id_type=pl.DeviceIdType.MESH)
    for copies in loads[:2]:
        for copy in copies:
            copy.start()

    def fine(src, dst):
        fine_step(src, mid, dst, fine_depth, retain)

    def coarse_rows(src, frame, row, size=group):
        start = row - frame
        h = raise_heights(
            take(src.at[0], start - 1, size + 2), take(src.at[1], start - 2, size + 2),
            take(src.at[1], start, size + 2), take(src.at[2], start - 1, size + 2),
            take(coarse_depth, row - 1, size + 2),
        )
        east, north = new_speeds(
            take(src.at[1], start, size), take(src.at[2], start, size), h[0:size],
            h[1 : size + 1], h[2 : size + 2], take(retain, row, size), coarse_courant,
        )
        return h[1 : size + 1], east, north

    def coarse(src, frame, dst, dst_frame, added=None, added_frame=0):
        def plus(value, field, row):
            if added is None:
                return value
            return value + take(added.at[field], row - added_frame, group)

        for r in range(0, rows, group):
            row = r + dst_frame
            start = row - frame
            mid[0, r : r + group] = raise_heights(
                take(src.at[0], start, group), take(src.at[1], start - 1, group),
                take(src.at[1], start + 1, group), take(src.at[2], start, group),
                take(coarse_depth, row, group),
            )
        for r in range(0, rows, group):
            row = r + dst_frame
            start = row - frame
            here = mid[0, r : r + group]
            east, north = new_speeds(
                take(src.at[1], start, group), take(src.at[2], start, group),
                take(mid.at[0], r - 1, group), here, take(mid.at[0], r + 1, group),
                take(retain, row, group), coarse_courant,
            )
            for field, value in enumerate((here, east, north)):
                dst[field, r : r + group] = plus(value, field, row)

    for copies in loads[:2]:
        for copy in copies:
            copy.wait()
    pl.semaphore_wait(barrier, len(partners))
    middle = own // 2
    mine = pl.ds(odd * middle, middle)
    theirs = pl.ds((1 - odd) * middle, middle)
    coef_copy = remote(
        raw.at[:, mine], raw_in.at[:, mine], coef_sems.at[0], coef_sems.at[1], (tm, other)
    )
    coef_share = remote(
        raw_in.at[:, mine], raw_in.at[:, mine], coef_sems.at[2], coef_sems.at[3], (sibling, sp)
    )
    coef_shared = remote(
        raw_in.at[:, theirs], raw_in.at[:, theirs], coef_sems.at[2], coef_sems.at[3], (sibling, sp)
    )
    coef_copy.start()
    for copies in loads[2:]:
        for copy in copies:
            copy.start()

    for copies in loads[2:4]:
        for copy in copies:
            copy.wait()

    def scaled(a):
        return jnp.concatenate([a[0:1] * height_scale, a[1:3]], axis=0)

    start_state = scaled(guess[...])
    ahead[...] = scaled(forcing[0]) - start_state
    ahead_copy = remote(ahead, ahead_in, ahead_sems.at[0], ahead_sems.at[1], (before, sp))
    ahead_copy.start()
    guess[...] = start_state
    track[0, :, 0:own] = start_state
    track[0, :, own:rows] = jnp.zeros((3, own, strips, lanes), jnp.float32)
    relax[0] = jnp.zeros((3, own, strips, lanes), jnp.float32)
    fine_depth[0:own] = (fine_courant * 0.5 * height_scale) * raw[0]
    coarse_depth[0:own] = (coarse_courant * 0.5 * height_scale) * raw[0]
    retain[0:own] = 1.0 - raw[1]
    coef_copy.wait_recv()
    coef_share.start()
    for copy in loads[4]:
        copy.wait()
    coef_copy.wait_send()
    coef_shared.wait_recv()
    coef_share.wait_send()
    fine_depth[own:rows] = (fine_courant * 0.5 * height_scale) * raw_in[0]
    coarse_depth[own:rows] = (coarse_courant * 0.5 * height_scale) * raw_in[0]
    retain[own:rows] = 1.0 - raw_in[1]

    def edge_copy(moment):
        return remote(
            edges.at[moment], edges_in.at[moment], edge_send.at[moment], edge_recv.at[moment],
            (tm, other),
        )

    def propagate(moment, carry):
        previous = moment - 1
        src = track.at[previous]
        dst = track.at[moment]
        fine(src, dst)
        for index, (ref, field) in enumerate(((src, 1), (mid, 0), (mid, 1), (dst, 0))):
            edges[previous, 2 * index] = ref[field, 0]
            edges[previous, 2 * index + 1] = ref[field, own - 1]

        @pl.when(previous < early_edges)
        def _():
            edge_copy(previous).start()

        dst[0, 0:own] += height_scale * forcing[moment, 0]
        dst[1, 0:own] += forcing[moment, 1]
        dst[2, 0:own] += forcing[moment, 2]
        return carry

    lax.fori_loop(1, moments, propagate, 0)
    fine(track.at[moments - 1], first)
    ahead_copy.wait()
    first[:, 0:own] += ahead_in[...]

    def bounded(ref, start, size, above, below):
        if start < 0:
            return jnp.concatenate([above[None], ref[0 : start + size]], axis=0)
        if start + size > own:
            return jnp.concatenate([ref[start:own], below[None]], axis=0)
        return ref[start : start + size]

    def relax_substep(src, dst, border, base):
        u_below, u_above = border[base], border[base + 1]
        h_below, h_above = border[base + 2], border[base + 3]
        for r in range(0, own, group):
            dst[0, r : r + group] = raise_heights(
                src[0, r : r + group], bounded(src.at[1], r - 1, group, u_above, u_below),
                bounded(src.at[1], r + 1, group, u_above, u_below), src[2, r : r + group],
                fine_depth[r : r + group],
            )
        for r in range(0, own, group):
            east, north = new_speeds(
                src[1, r : r + group], src[2, r : r + group],
                bounded(dst.at[0], r - 1, group, h_above, h_below), dst[0, r : r + group],
                bounded(dst.at[0], r + 1, group, h_above, h_below), retain[r : r + group],
                fine_courant,
            )
            dst[1, r : r + group] = east
            dst[2, r : r + group] = north

    def relaxed(low, high):
        def step(moment, carry):
            previous = moment - 1
            edge_copy(previous).wait()
            border = edges_in.at[previous]
            a = previous % 2
            b = moment % 2
            relax_substep(relax.at[a], relax_mid, border, 0)
            relax_substep(relax_mid, relax.at[b], border, 4)
            track[moment, :, 0:own] += relax[b]
            return carry

        lax.fori_loop(low, high, step, 0)

    def late_edges():
        def step(moment, carry):
            edge_copy(moment).start()
            return carry

        lax.fori_loop(early_edges, moments - 1, step, 0)

    def span(index):
        return pl.ds(index * piece, piece)

    lift_pieces = rows // lift_piece
    lift_order = [(index + lift_pieces // 2) % lift_pieces for index in range(lift_pieces)]

    def lift_copy(index):
        here = pl.ds(index * lift_piece, lift_piece)
        return remote(
            lift.at[:, here], lift_in.at[:, here], lift_send.at[index], lift_recv.at[index],
            (sibling, sp),
        )

    here_copy = remote(lower, lower_here, here_sems.at[0], here_sems.at[1], (sibling, sp))
    own_copy = remote(
        second.at[chip, :, 0:own], own_in, own_sems.at[0], own_sems.at[1], (sibling, sp)
    )
    passed_copy = remote(passed, passed_in, passed_sems.at[0], passed_sems.at[1], (after_chip, sp))
    lower_copies = [
        remote(
            first.at[:, start : start + own], lower_in.at[:, own - start : rows - start],
            lower_send.at[index], lower_recv.at[1 - index], (tm, other),
        )
        for index, start in enumerate((0, own))
    ]
    top_frame = 4
    wave_pieces = ((0, own), (own, rows - top_frame), (rows - top_frame, rows))
    wave_copies = [
        remote(
            climb.at[1, :, start:end], wave.at[0, :, (start + top_frame) % rows : (end + top_frame - 1) % rows + 1],
            wave_send.at[index], wave_recv.at[index], (sibling, sp),
        )
        for index, (start, end) in enumerate(wave_pieces)
    ]

    def part_copy(index):
        landing = (index + chunks // 2) % chunks
        return remote(
            part.at[:, span(index)], part_in.at[:, span(landing)], part_send.at[index],
            part_recv.at[landing], (tm, other),
        )

    def exchange(ref, slot, send, recv, to):
        def copy(index):
            return remote(
                ref.at[slot, :, span(index)], ref.at[slot, :, span(index)], send.at[index],
                recv.at[index], (to, sp),
            )

        return copy

    second_copy = exchange(second, chip, second_send, second_recv, facing)
    second_in = exchange(second, 1 - chip, second_send, second_recv, facing)
    third_copy = exchange(third, pair, third_send, third_recv, beside)
    third_in = exchange(third, 1 - pair, third_send, third_recv, beside)
    fourth_copy = exchange(fourth, half, fourth_send, fourth_recv, inward)
    fourth_in = exchange(fourth, 1 - half, relay_send, fourth_recv, beside)

    @pl.when(odd == 0)
    def _():
        for index in lift_order:
            start = index * lift_piece
            values = coarse_rows(first, 0, start, lift_piece)
            for field in range(3):
                lift[field, start : start + lift_piece] = values[field]
            lift_copy(index).start()
        relaxed(1, early_edges + 1)
        pl.semaphore_wait(go_sem, 1)
        for copy in lower_copies:
            copy.start()
        late_edges()
        own_copy.wait_recv()
        for copy in lower_copies:
            copy.wait()
        lower[...] = first[...] + lower_in[...]
        here_copy.start()
        for r in range(0, own, group):
            values = coarse_rows(lower, 0, r)
            for field in range(3):
                passed[field, r : r + group] = own_in[field, r : r + group] - values[field]
        passed_copy.start()
        relaxed(early_edges + 1, moments)
        for index in lift_order:
            lift_copy(index).wait_send()
        passed_copy.wait()
        here_copy.wait_send()
        for copy in wave_copies:
            copy.wait_recv()

    @pl.when(odd == 1)
    def _():
        for index in lift_order:
            lift_copy(index).wait_recv()
            for inside in range(lift_piece // piece):
                chunk = index * (lift_piece // piece) + inside
                here = slice(chunk * piece, (chunk + 1) * piece)
                part[:, here] = first[:, here] + lift_in[:, here]
                part_copy(chunk).start()
        late_edges()
        relaxed(1, early_edges + 1)

        for index in range(chunks):
            here = slice(index * piece, (index + 1) * piece)
            part_copy((index + chunks // 2) % chunks).wait_recv()
            second[chip, :, here] = part[:, here] + part_in[:, here]
            second_copy(index).start()
            if index == chunks // 2:
                pl.semaphore_signal(
                    go_sem, inc=1, device_id=(sibling, sp), device_id_type=pl.DeviceIdType.MESH
                )

        own_copy.start()

        def ascend(src, arriving, frame, dst, slot, sent, sends):
            for index in range(chunks):
                if index == 0:
                    arriving(0).wait_recv()
                    arriving(1).wait_recv()
                if index + 2 < chunks:
                    arriving(index + 2).wait_recv()
                values = coarse_rows(src.at[0], frame, index * piece + frame + 2, piece)
                for field in range(3):
                    dst[slot, field, index * piece : (index + 1) * piece] = values[field] + take(
                        src.at[1, field], index * piece + 2, piece
                    )
                if sends is None:
                    sent(index).start()
                else:
                    @pl.when(sends)
                    def _():
                        sent(index).start()

        ascend(second, second_in, 0, third, pair, third_copy, None)
        ascend(third, third_in, 2, fourth, half, fourth_copy, inner)

        @pl.when(jnp.logical_not(inner))
        def _():
            relaxed(early_edges + 1, moments)

        for index in range(chunks):
            fourth_in(index).wait_recv()

            @pl.when(inner)
            def _():
                fourth_in(index).start()

        @pl.when(inner)
        def _():
            relaxed(early_edges + 1, moments)

        coarse(fourth.at[0], 4, climb.at[0], 4, fourth.at[1], 4)
        coarse(climb.at[0], 4, climb.at[1], 4, climb.at[0], 4)

        def rise(bit, src, dst, added, added_frame):
            @pl.when(bit == 1)
            def _():
                coarse(src, 4, dst, 4, added, added_frame)

            @pl.when(bit == 0)
            def _():
                dst[...] = src[...]

        rise(half, climb.at[1], climb.at[0], fourth.at[0], 4)
        rise(pair, climb.at[0], climb.at[2], third.at[0], 2)

        for (start, end), copy in zip(wave_pieces, wave_copies):
            @pl.when(chip == 1)
            def _():
                values = coarse_rows(climb.at[2], 4, start + 4, end - start)
                for field in range(3):
                    climb[1, field, start:end] = values[field] + take(
                        second.at[0, field], start + 4, end - start
                    )

            @pl.when(chip == 0)
            def _():
                climb[1, :, start:end] = climb[2, :, start:end]

            copy.start()
        here_copy.wait_recv()
        coarse(climb.at[1], 4, wave.at[0], 0, lower_here, 0)

        own_copy.wait_send()
        for index in range(chunks):
            part_copy(index).wait_send()
            second_copy(index).wait_send()
            third_copy(index).wait_send()

            @pl.when(inner)
            def _():
                fourth_copy(index).wait_send()
                fourth_in(index).wait_send()

        for copy in wave_copies:
            copy.wait_send()

    corrected[...] = wave[0]

    @pl.when(odd == 1)
    def _():
        own_part[...] = lower_here[:, 0:own]

    @pl.when(odd == 0)
    def _():
        own_part[...] = passed_in[...]


def finish_kernel(
    track, corrected, own_part, fine_depth, retain, out, residual, wave, mid, ready, ready_part, out_sems
):
    moments, _, own, strips, _ = ready.shape

    def store(src, dst, index):
        return [
            pltpu.make_async_copy(
                src.at[:, :, strip, :], dst.at[:, :, pl.ds(strip * lanes, lanes)],
                out_sems.at[index, strip],
            )
            for strip in range(strips)
        ]

    ready_part[0] = own_part[0] * (1.0 / height_scale)
    ready_part[1:3] = own_part[1:3]
    for copy in store(ready_part, residual.at[0], moments):
        copy.start()

    def finish(moment, values):
        ready[moment, 0] = (1.0 / height_scale) * (values[0] + track[moment, 0, 0:own])
        ready[moment, 1] = values[1] + track[moment, 1, 0:own]
        ready[moment, 2] = values[2] + track[moment, 2, 0:own]
        for copy in store(ready.at[moment], out.at[moment], moment):
            copy.start()

    wave[0] = corrected[...]
    finish(0, corrected[:, 0:own])

    def correct(moment, carry):
        a = (moment - 1) % 2
        b = moment % 2
        fine_step(wave.at[a], mid, wave.at[b], fine_depth, retain)
        finish(moment, wave[b, :, 0:own])
        return carry

    lax.fori_loop(1, moments, correct, 0)

    def drain(moment, carry):
        for copy in store(ready.at[moment], out.at[moment], moment):
            copy.wait()
        return carry

    lax.fori_loop(0, moments, drain, 0)
    for copy in store(ready_part, residual.at[0], moments):
        copy.wait()


def kernel_body(cpoint_guess, tide_forcing, depth, drag):
    moments, fields, own, cols = tide_forcing.shape
    strips = cols // lanes
    rows = 2 * own
    chunks = rows // piece

    def held(*shape):
        return pltpu.VMEM((*shape, strips, lanes), jnp.float32)

    dma = pltpu.SemaphoreType.DMA
    vmem = pl.BlockSpec(memory_space=pltpu.VMEM)
    def given(*shape):
        return jax.ShapeDtypeStruct((*shape, strips, lanes), jnp.float32)

    hbm = pl.BlockSpec(memory_space=pltpu.HBM)
    passed_on = pl.pallas_call(
        cycle_kernel,
        out_shape=(
            given(moments, fields, rows),
            given(fields, rows),
            given(fields, own),
            given(rows),
            given(rows),
        ),
        in_specs=[hbm] * 4,
        out_specs=(vmem,) * 5,
        scratch_shapes=[
            held(fields, own),
            held(moments, fields, own),
            held(2, own),
            held(2, own),
            held(rows),
            held(fields, rows),
            held(moments - 1, 8),
            held(moments - 1, 8),
            held(fields, own),
            held(fields, own),
            held(fields, rows),
            held(fields, rows),
            held(fields, rows),
            held(fields, rows),
            held(fields, rows),
            held(2, fields, rows),
            held(2, fields, rows),
            held(2, fields, rows),
            held(3, fields, rows),
            held(2, fields, rows),
            held(fields, rows),
            held(fields, rows),
            held(fields, rows),
            held(fields, own),
            held(fields, own),
            held(fields, own),
            held(2, fields, own),
            held(fields, own),
            dma((5, strips)),
            dma((4,)),
            dma((2,)),
            dma((moments - 1,)),
            dma((moments - 1,)),
            dma((rows // lift_piece,)),
            dma((rows // lift_piece,)),
            dma((chunks,)),
            dma((chunks,)),
            dma((chunks,)),
            dma((chunks,)),
            dma((chunks,)),
            dma((chunks,)),
            dma((chunks,)),
            dma((chunks,)),
            dma((chunks,)),
            dma((2,)),
            dma((2,)),
            dma((2,)),
            dma((2,)),
            dma((2,)),
            dma((3,)),
            dma((3,)),
            pltpu.SemaphoreType.REGULAR,
        ],
        compiler_params=pltpu.CompilerParams(
            collective_id=0, has_side_effects=True, vmem_limit_bytes=32 * 1024 * 1024
        ),
    )(*(
        pltpu.with_memory_space_constraint(array, pltpu.HBM)
        for array in (cpoint_guess, tide_forcing, depth, drag)
    ))
    return pl.pallas_call(
        finish_kernel,
        out_shape=(
            jax.ShapeDtypeStruct(tide_forcing.shape, jnp.float32),
            jax.ShapeDtypeStruct(cpoint_guess.shape, jnp.float32),
        ),
        in_specs=[vmem] * 5,
        out_specs=(hbm, hbm),
        scratch_shapes=[
            held(2, fields, rows),
            held(fields, rows),
            held(moments, fields, own),
            held(fields, own),
            dma((moments + 1, strips)),
        ],
        compiler_params=pltpu.CompilerParams(vmem_limit_bytes=16 * 1024 * 1024),
    )(*passed_on)


def solution(mesh):
    placed = (
        P("tm", None, "space", None),
        P("tm", None, "space", None),
        P("space", None),
        P("space", None),
    )
    one_top_point = mesh.shape["tm"] == 2 ** (LEVELS - 1)
    fits = one_top_point and mesh.shape["space"] == 2
    return jax.shard_map(
        kernel_body if fits else body,
        mesh=mesh,
        in_specs=placed,
        out_specs=(P("tm", None, "space", None), P("tm", None, "space", None)),
        check_vma=False,
    )
```

```python
import jax
import jax.numpy as jnp
from jax import lax
from jax.experimental import pallas as pl
from jax.experimental.pallas import tpu as pltpu
from jax.sharding import PartitionSpec as P

LEVELS = 5


coriolis = 0.1
fine_courant = 0.25
coarse_courant = 0.5


def with_halo(cells, sides, width):
    for axis, dim in sides:
        count = lax.axis_size(axis)
        head = lax.slice_in_dim(cells, 0, width, axis=dim)
        tail = lax.slice_in_dim(cells, cells.shape[dim] - width, cells.shape[dim], axis=dim)
        cells = jnp.concatenate(
            [
                lax.ppermute(tail, axis, [(i, (i + 1) % count) for i in range(count)]),
                cells,
                lax.ppermute(head, axis, [((i + 1) % count, i) for i in range(count)]),
            ],
            axis=dim,
        )
    return cells


def shifted(block, axis, distance):
    devices = range(lax.axis_size(axis))
    route = [((i - distance) % len(devices), i) for i in devices]
    return lax.ppermute(block, axis, route)


def across_rows(field):
    return (field[2:] - field[:-2]) * 0.5


def along_cols(field):
    return (jnp.roll(field, -1, -1) - jnp.roll(field, 1, -1)) * 0.5


def advance(padded, coefficients, courant):
    height = padded[0]
    eastward = padded[1]
    northward = padded[2]
    new_height = height[1:-1] - courant * coefficients[0, 1:-1] * (
        across_rows(eastward) + along_cols(northward)[1:-1]
    )
    retain = 1.0 - coefficients[1, 2:-2]
    east_middle = eastward[2:-2]
    north_middle = northward[2:-2]
    new_east = (
        retain * east_middle + courant * coriolis * north_middle - courant * across_rows(new_height)
    )
    new_north = (
        retain * north_middle
        - courant * coriolis * east_middle
        - courant * along_cols(new_height)[1:-1]
    )
    return jnp.stack((new_height[1:-1], new_east, new_north))


def body(cpoint_guess, tide_forcing, depth, drag):
    coefficients = with_halo(jnp.stack((depth, drag)), (("space", 1),), 4)
    narrow = coefficients[:, 2:-2]

    def one_substep(state, courant):
        padded = with_halo(state, (("space", 1),), 2)
        return advance(padded, narrow, courant)

    def fine_map(state):
        padded = with_halo(state, (("space", 1),), 4)
        middle = advance(padded, coefficients, fine_courant)
        result = advance(middle, narrow, fine_courant)
        return result

    def coarse_map(state):
        return one_substep(state, coarse_courant)

    def pass_on(state, stride, mapper):
        result = shifted(mapper(state), "tm", stride)
        return result

    start = cpoint_guess[0]
    state = start
    for moment in range(1, tide_forcing.shape[0]):
        state = fine_map(state) + tide_forcing[moment]
    right = pass_on(state, 1, fine_map) + tide_forcing[0] - start
    rights = [right]
    for level in range(1, LEVELS):
        current = rights[-1]
        rights.append(current + pass_on(current, 2 ** (level - 1), coarse_map))
    top_stride = 2 ** (LEVELS - 1)
    points = lax.axis_size("tm") // top_stride
    position = lax.axis_index("tm")
    base = rights[-1]
    anchor = position % top_stride == 0

    def sweep(counter, correction):
        arrived = pass_on(correction, top_stride, coarse_map)
        target = jnp.logical_and(anchor, position // top_stride == counter % points)
        return jnp.where(target, arrived + base, correction)

    correction = lax.fori_loop(1, points + 1, sweep, base)
    for level in range(LEVELS - 1, 0, -1):
        stride = 2 ** (level - 1)
        arrived = pass_on(correction, stride, coarse_map)
        odd_point = position % (2 * stride) == stride
        correction = jnp.where(odd_point, arrived + rights[level - 1], correction)
    state = start + correction
    states = [state]
    for moment in range(1, tide_forcing.shape[0]):
        state = fine_map(state) + tide_forcing[moment]
        states.append(state)
    return (jnp.stack(states), right[None])


lanes = 128
group = 4
piece = 4
lift_piece = 8
ahead_pieces = 4 // piece
height_scale = 0.125
early_edges = 3


def down_cols(a):
    here = lax.broadcasted_iota(jnp.int32, a.shape, 2)
    following = jnp.where(here == 0, pltpu.roll(a, a.shape[1] - 1, 1), a)
    preceding = jnp.where(here == lanes - 1, pltpu.roll(a, 1, 1), a)
    return pltpu.roll(following, lanes - 1, 2) - pltpu.roll(preceding, 1, 2)


def take(ref, start, size):
    total = ref.shape[0]
    start %= total
    if start + size <= total:
        return ref[start : start + size]
    return jnp.concatenate([ref[start:total], ref[0 : start + size - total]], axis=0)


def raise_heights(h, u_before, u_after, v, depths):
    return h - depths * (u_after - u_before + down_cols(v))


def new_speeds(u, v, h_before, h, h_after, kept, courant):
    turn = courant * coriolis
    east = h_after - h_before
    north = down_cols(h)
    slope = courant * 0.5 / height_scale
    if slope != 1.0:
        east = slope * east
        north = slope * north
    return kept * u + turn * v - east, kept * v - turn * u - north


def fine_substep(src, dst, depths, kept):
    rows = src.shape[1]
    for r in range(0, rows, group):
        dst[0, r : r + group] = raise_heights(
            src[0, r : r + group], take(src.at[1], r - 1, group), take(src.at[1], r + 1, group),
            src[2, r : r + group], depths[r : r + group],
        )
    for r in range(0, rows, group):
        east, north = new_speeds(
            src[1, r : r + group], src[2, r : r + group], take(dst.at[0], r - 1, group),
            dst[0, r : r + group], take(dst.at[0], r + 1, group), kept[r : r + group],
            fine_courant,
        )
        dst[1, r : r + group] = east
        dst[2, r : r + group] = north


def fine_step(src, middle, dst, depths, kept):
    fine_substep(src, middle, depths, kept)
    fine_substep(middle, dst, depths, kept)


def cycle_kernel(
    guess_hbm, forcing_hbm, depth_hbm, drag_hbm, track, corrected, own_part, fine_depth, retain,
    guess, forcing, raw, raw_in, coarse_depth, mid, edges, edges_in,
    ahead, ahead_in, first, lift, lift_in, part, part_in, second, third, fourth, climb, wave,
    lower_in, lower, lower_here, own_in, passed, passed_in, relax, relax_mid,
    load_sems, coef_sems, ahead_sems, edge_send, edge_recv, lift_send, lift_recv, part_send, part_recv,
    second_send, second_recv, third_send, third_recv, fourth_send, fourth_recv, relay_send,
    lower_send, lower_recv, here_sems, own_sems, passed_sems, wave_send, wave_recv, go_sem,
):
    tm = lax.axis_index("tm")
    sp = lax.axis_index("space")
    count = lax.axis_size("tm")
    moments = forcing.shape[0]
    own = guess.shape[1]
    rows = 2 * own
    strips = guess.shape[2]
    chunks = rows // piece
    other = 1 - sp
    odd = tm % 2
    chip = (tm // 2) % 2
    layer = tm // 4
    pair = layer % 2
    half = layer // 2
    before = (tm + count - 1) % count
    after_chip = (tm + 2) % count
    sibling = tm + 1 - 2 * odd
    facing = tm + 2 - 4 * chip
    beside = tm + 4 - 8 * pair
    inner = pair != half
    inward = (tm + 4 - 8 * half + count) % count

    def load(src, dst, index):
        return [
            pltpu.make_async_copy(
                src.at[..., pl.ds(strip * lanes, lanes)], dst.at[..., strip, :],
                load_sems.at[index, strip],
            )
            for strip in range(strips)
        ]

    loads = [
        load(depth_hbm, raw.at[0], 0),
        load(drag_hbm, raw.at[1], 1),
        load(guess_hbm.at[0], guess, 2),
        load(forcing_hbm.at[0], forcing.at[0], 3),
        load(forcing_hbm.at[1:moments], forcing.at[1:moments], 4),
    ]

    def remote(src, dst, send, recv, to):
        return pltpu.make_async_remote_copy(
            src_ref=src, dst_ref=dst, send_sem=send, recv_sem=recv,
            device_id=to, device_id_type=pl.DeviceIdType.MESH,
        )

    barrier = pltpu.get_barrier_semaphore()
    partners = [(tm, other)]
    for distance in (1, 2, 4):
        partners.append(((tm + distance) % count, sp))
        partners.append(((tm + count - distance) % count, sp))
    for to in partners:
        pl.semaphore_signal(barrier, inc=1, device_id=to, device_id_type=pl.DeviceIdType.MESH)
    for copies in loads[:2]:
        for copy in copies:
            copy.start()

    def fine(src, dst):
        fine_step(src, mid, dst, fine_depth, retain)

    def coarse_rows(src, frame, row, size=group):
        start = row - frame
        h = raise_heights(
            take(src.at[0], start - 1, size + 2), take(src.at[1], start - 2, size + 2),
            take(src.at[1], start, size + 2), take(src.at[2], start - 1, size + 2),
            take(coarse_depth, row - 1, size + 2),
        )
        east, north = new_speeds(
            take(src.at[1], start, size), take(src.at[2], start, size), h[0:size],
            h[1 : size + 1], h[2 : size + 2], take(retain, row, size), coarse_courant,
        )
        return h[1 : size + 1], east, north

    def coarse(src, frame, dst, dst_frame, added=None, added_frame=0):
        def plus(value, field, row):
            if added is None:
                return value
            return value + take(added.at[field], row - added_frame, group)

        for r in range(0, rows, group):
            row = r + dst_frame
            start = row - frame
            mid[0, r : r + group] = raise_heights(
                take(src.at[0], start, group), take(src.at[1], start - 1, group),
                take(src.at[1], start + 1, group), take(src.at[2], start, group),
                take(coarse_depth, row, group),
            )
        for r in range(0, rows, group):
            row = r + dst_frame
            start = row - frame
            here = mid[0, r : r + group]
            east, north = new_speeds(
                take(src.at[1], start, group), take(src.at[2], start, group),
                take(mid.at[0], r - 1, group), here, take(mid.at[0], r + 1, group),
                take(retain, row, group), coarse_courant,
            )
            for field, value in enumerate((here, east, north)):
                dst[field, r : r + group] = plus(value, field, row)

    for copies in loads[:2]:
        for copy in copies:
            copy.wait()
    pl.semaphore_wait(barrier, len(partners))
    middle = own // 2
    mine = pl.ds(odd * middle, middle)
    theirs = pl.ds((1 - odd) * middle, middle)
    coef_copy = remote(
        raw.at[:, mine], raw_in.at[:, mine], coef_sems.at[0], coef_sems.at[1], (tm, other)
    )
    coef_share = remote(
        raw_in.at[:, mine], raw_in.at[:, mine], coef_sems.at[2], coef_sems.at[3], (sibling, sp)
    )
    coef_shared = remote(
        raw_in.at[:, theirs], raw_in.at[:, theirs], coef_sems.at[2], coef_sems.at[3], (sibling, sp)
    )
    coef_copy.start()
    for copies in loads[2:]:
        for copy in copies:
            copy.start()

    for copies in loads[2:4]:
        for copy in copies:
            copy.wait()

    def scaled(a):
        return jnp.concatenate([a[0:1] * height_scale, a[1:3]], axis=0)

    start_state = scaled(guess[...])
    ahead[...] = scaled(forcing[0]) - start_state
    ahead_copy = remote(ahead, ahead_in, ahead_sems.at[0], ahead_sems.at[1], (before, sp))
    ahead_copy.start()
    guess[...] = start_state
    track[0, :, 0:own] = start_state
    track[0, :, own:rows] = jnp.zeros((3, own, strips, lanes), jnp.float32)
    relax[0] = jnp.zeros((3, own, strips, lanes), jnp.float32)
    fine_depth[0:own] = (fine_courant * 0.5 * height_scale) * raw[0]
    coarse_depth[0:own] = (coarse_courant * 0.5 * height_scale) * raw[0]
    retain[0:own] = 1.0 - raw[1]
    coef_copy.wait_recv()
    coef_share.start()
    for copy in loads[4]:
        copy.wait()
    coef_copy.wait_send()
    coef_shared.wait_recv()
    coef_share.wait_send()
    fine_depth[own:rows] = (fine_courant * 0.5 * height_scale) * raw_in[0]
    coarse_depth[own:rows] = (coarse_courant * 0.5 * height_scale) * raw_in[0]
    retain[own:rows] = 1.0 - raw_in[1]

    def edge_copy(moment):
        return remote(
            edges.at[moment], edges_in.at[moment], edge_send.at[moment], edge_recv.at[moment],
            (tm, other),
        )

    def propagate(moment, carry):
        previous = moment - 1
        src = track.at[previous]
        dst = track.at[moment]
        fine(src, dst)
        for index, (ref, field) in enumerate(((src, 1), (mid, 0), (mid, 1), (dst, 0))):
            edges[previous, 2 * index] = ref[field, 0]
            edges[previous, 2 * index + 1] = ref[field, own - 1]

        @pl.when(previous < early_edges)
        def _():
            edge_copy(previous).start()

        dst[0, 0:own] += height_scale * forcing[moment, 0]
        dst[1, 0:own] += forcing[moment, 1]
        dst[2, 0:own] += forcing[moment, 2]
        return carry

    lax.fori_loop(1, moments, propagate, 0)
    fine(track.at[moments - 1], first)
    ahead_copy.wait()
    first[:, 0:own] += ahead_in[...]

    def bounded(ref, start, size, above, below):
        if start < 0:
            return jnp.concatenate([above[None], ref[0 : start + size]], axis=0)
        if start + size > own:
            return jnp.concatenate([ref[start:own], below[None]], axis=0)
        return ref[start : start + size]

    def relax_substep(src, dst, border, base):
        u_below, u_above = border[base], border[base + 1]
        h_below, h_above = border[base + 2], border[base + 3]
        for r in range(0, own, group):
            dst[0, r : r + group] = raise_heights(
                src[0, r : r + group], bounded(src.at[1], r - 1, group, u_above, u_below),
                bounded(src.at[1], r + 1, group, u_above, u_below), src[2, r : r + group],
                fine_depth[r : r + group],
            )
        for r in range(0, own, group):
            east, north = new_speeds(
                src[1, r : r + group], src[2, r : r + group],
                bounded(dst.at[0], r - 1, group, h_above, h_below), dst[0, r : r + group],
                bounded(dst.at[0], r + 1, group, h_above, h_below), retain[r : r + group],
                fine_courant,
            )
            dst[1, r : r + group] = east
            dst[2, r : r + group] = north

    def relaxed(low, high):
        def step(moment, carry):
            previous = moment - 1
            edge_copy(previous).wait()
            border = edges_in.at[previous]
            a = previous % 2
            b = moment % 2
            relax_substep(relax.at[a], relax_mid, border, 0)
            relax_substep(relax_mid, relax.at[b], border, 4)
            track[moment, :, 0:own] += relax[b]
            return carry

        lax.fori_loop(low, high, step, 0)

    def late_edges():
        def step(moment, carry):
            edge_copy(moment).start()
            return carry

        lax.fori_loop(early_edges, moments - 1, step, 0)

    def span(index):
        return pl.ds(index * piece, piece)

    lift_pieces = rows // lift_piece
    lift_order = [(index + lift_pieces // 2) % lift_pieces for index in range(lift_pieces)]

    def lift_copy(index):
        here = pl.ds(index * lift_piece, lift_piece)
        return remote(
            lift.at[:, here], lift_in.at[:, here], lift_send.at[index], lift_recv.at[index],
            (sibling, sp),
        )

    here_copy = remote(lower, lower_here, here_sems.at[0], here_sems.at[1], (sibling, sp))
    own_copy = remote(
        second.at[chip, :, 0:own], own_in, own_sems.at[0], own_sems.at[1], (sibling, sp)
    )
    passed_copy = remote(passed, passed_in, passed_sems.at[0], passed_sems.at[1], (after_chip, sp))
    lower_copies = [
        remote(
            first.at[:, start : start + own], lower_in.at[:, own - start : rows - start],
            lower_send.at[index], lower_recv.at[1 - index], (tm, other),
        )
        for index, start in enumerate((0, own))
    ]
    top_frame = 4
    wave_pieces = ((0, own), (own, rows - top_frame), (rows - top_frame, rows))
    wave_copies = [
        remote(
            climb.at[1, :, start:end], wave.at[0, :, (start + top_frame) % rows : (end + top_frame - 1) % rows + 1],
            wave_send.at[index], wave_recv.at[index], (sibling, sp),
        )
        for index, (start, end) in enumerate(wave_pieces)
    ]

    def part_copy(index):
        landing = (index + chunks // 2) % chunks
        return remote(
            part.at[:, span(index)], part_in.at[:, span(landing)], part_send.at[index],
            part_recv.at[landing], (tm, other),
        )

    def exchange(ref, slot, send, recv, to):
        def copy(index):
            return remote(
                ref.at[slot, :, span(index)], ref.at[slot, :, span(index)], send.at[index],
                recv.at[index], (to, sp),
            )

        return copy

    second_copy = exchange(second, chip, second_send, second_recv, facing)
    second_in = exchange(second, 1 - chip, second_send, second_recv, facing)
    third_copy = exchange(third, pair, third_send, third_recv, beside)
    third_in = exchange(third, 1 - pair, third_send, third_recv, beside)
    fourth_copy = exchange(fourth, half, fourth_send, fourth_recv, inward)
    fourth_in = exchange(fourth, 1 - half, relay_send, fourth_recv, beside)

    @pl.when(odd == 0)
    def _():
        for index in lift_order:
            start = index * lift_piece
            values = coarse_rows(first, 0, start, lift_piece)
            for field in range(3):
                lift[field, start : start + lift_piece] = values[field]
            lift_copy(index).start()
        relaxed(1, early_edges + 1)
        pl.semaphore_wait(go_sem, 1)
        for copy in lower_copies:
            copy.start()
        late_edges()
        own_copy.wait_recv()
        for copy in lower_copies:
            copy.wait()
        lower[...] = first[...] + lower_in[...]
        here_copy.start()
        for r in range(0, own, group):
            values = coarse_rows(lower, 0, r)
            for field in range(3):
                passed[field, r : r + group] = own_in[field, r : r + group] - values[field]
        passed_copy.start()
        relaxed(early_edges + 1, moments)
        for index in lift_order:
            lift_copy(index).wait_send()
        passed_copy.wait()
        here_copy.wait_send()
        for copy in wave_copies:
            copy.wait_recv()

    @pl.when(odd == 1)
    def _():
        for index in lift_order:
            lift_copy(index).wait_recv()
            for inside in range(lift_piece // piece):
                chunk = index * (lift_piece // piece) + inside
                here = slice(chunk * piece, (chunk + 1) * piece)
                part[:, here] = first[:, here] + lift_in[:, here]
                part_copy(chunk).start()
        late_edges()
        relaxed(1, early_edges + 1)

        for index in range(chunks):
            here = slice(index * piece, (index + 1) * piece)
            part_copy((index + chunks // 2) % chunks).wait_recv()
            second[chip, :, here] = part[:, here] + part_in[:, here]
            second_copy(index).start()
            if index == chunks // 2:
                pl.semaphore_signal(
                    go_sem, inc=1, device_id=(sibling, sp), device_id_type=pl.DeviceIdType.MESH
                )

        own_copy.start()

        def ascend(src, arriving, frame, dst, slot, sent, sends):
            for index in range(chunks):
                if index == 0:
                    arriving(0).wait_recv()
                    if piece < 4:
                        arriving(1).wait_recv()
                if index + ahead_pieces < chunks:
                    arriving(index + ahead_pieces).wait_recv()
                values = coarse_rows(src.at[0], frame, index * piece + frame + 2, piece)
                for field in range(3):
                    dst[slot, field, index * piece : (index + 1) * piece] = values[field] + take(
                        src.at[1, field], index * piece + 2, piece
                    )
                if sends is None:
                    sent(index).start()
                else:
                    @pl.when(sends)
                    def _():
                        sent(index).start()

        ascend(second, second_in, 0, third, pair, third_copy, None)
        ascend(third, third_in, 2, fourth, half, fourth_copy, inner)

        @pl.when(jnp.logical_not(inner))
        def _():
            relaxed(early_edges + 1, moments)

        for index in range(chunks):
            fourth_in(index).wait_recv()

            @pl.when(inner)
            def _():
                fourth_in(index).start()

        @pl.when(inner)
        def _():
            relaxed(early_edges + 1, moments)

        coarse(fourth.at[0], 4, climb.at[0], 4, fourth.at[1], 4)
        coarse(climb.at[0], 4, climb.at[1], 4, climb.at[0], 4)

        def rise(bit, src, dst, added, added_frame):
            @pl.when(bit == 1)
            def _():
                coarse(src, 4, dst, 4, added, added_frame)

            @pl.when(bit == 0)
            def _():
                dst[...] = src[...]

        rise(half, climb.at[1], climb.at[0], fourth.at[0], 4)
        rise(pair, climb.at[0], climb.at[2], third.at[0], 2)

        for (start, end), copy in zip(wave_pieces, wave_copies):
            @pl.when(chip == 1)
            def _():
                values = coarse_rows(climb.at[2], 4, start + 4, end - start)
                for field in range(3):
                    climb[1, field, start:end] = values[field] + take(
                        second.at[0, field], start + 4, end - start
                    )

            @pl.when(chip == 0)
            def _():
                climb[1, :, start:end] = climb[2, :, start:end]

            copy.start()
        here_copy.wait_recv()
        coarse(climb.at[1], 4, wave.at[0], 0, lower_here, 0)

        own_copy.wait_send()
        for index in range(chunks):
            part_copy(index).wait_send()
            second_copy(index).wait_send()
            third_copy(index).wait_send()

            @pl.when(inner)
            def _():
                fourth_copy(index).wait_send()
                fourth_in(index).wait_send()

        for copy in wave_copies:
            copy.wait_send()

    corrected[...] = wave[0]

    @pl.when(odd == 1)
    def _():
        own_part[...] = lower_here[:, 0:own]

    @pl.when(odd == 0)
    def _():
        own_part[...] = passed_in[...]


def finish_kernel(
    track, corrected, own_part, fine_depth, retain, out, residual, wave, mid, ready, ready_part, out_sems
):
    moments, _, own, strips, _ = ready.shape

    def store(src, dst, index):
        return [
            pltpu.make_async_copy(
                src.at[:, :, strip, :], dst.at[:, :, pl.ds(strip * lanes, lanes)],
                out_sems.at[index, strip],
            )
            for strip in range(strips)
        ]

    ready_part[0] = own_part[0] * (1.0 / height_scale)
    ready_part[1:3] = own_part[1:3]
    for copy in store(ready_part, residual.at[0], moments):
        copy.start()

    def finish(moment, values):
        ready[moment, 0] = (1.0 / height_scale) * (values[0] + track[moment, 0, 0:own])
        ready[moment, 1] = values[1] + track[moment, 1, 0:own]
        ready[moment, 2] = values[2] + track[moment, 2, 0:own]
        for copy in store(ready.at[moment], out.at[moment], moment):
            copy.start()

    wave[0] = corrected[...]
    finish(0, corrected[:, 0:own])

    def correct(moment, carry):
        a = (moment - 1) % 2
        b = moment % 2
        fine_step(wave.at[a], mid, wave.at[b], fine_depth, retain)
        finish(moment, wave[b, :, 0:own])
        return carry

    lax.fori_loop(1, moments, correct, 0)

    def drain(moment, carry):
        for copy in store(ready.at[moment], out.at[moment], moment):
            copy.wait()
        return carry

    lax.fori_loop(0, moments, drain, 0)
    for copy in store(ready_part, residual.at[0], moments):
        copy.wait()


def kernel_body(cpoint_guess, tide_forcing, depth, drag):
    moments, fields, own, cols = tide_forcing.shape
    strips = cols // lanes
    rows = 2 * own
    chunks = rows // piece

    def held(*shape):
        return pltpu.VMEM((*shape, strips, lanes), jnp.float32)

    dma = pltpu.SemaphoreType.DMA
    vmem = pl.BlockSpec(memory_space=pltpu.VMEM)
    def given(*shape):
        return jax.ShapeDtypeStruct((*shape, strips, lanes), jnp.float32)

    hbm = pl.BlockSpec(memory_space=pltpu.HBM)
    passed_on = pl.pallas_call(
        cycle_kernel,
        out_shape=(
            given(moments, fields, rows),
            given(fields, rows),
            given(fields, own),
            given(rows),
            given(rows),
        ),
        in_specs=[hbm] * 4,
        out_specs=(vmem,) * 5,
        scratch_shapes=[
            held(fields, own),
            held(moments, fields, own),
            held(2, own),
            held(2, own),
            held(rows),
            held(fields, rows),
            held(moments - 1, 8),
            held(moments - 1, 8),
            held(fields, own),
            held(fields, own),
            held(fields, rows),
            held(fields, rows),
            held(fields, rows),
            held(fields, rows),
            held(fields, rows),
            held(2, fields, rows),
            held(2, fields, rows),
            held(2, fields, rows),
            held(3, fields, rows),
            held(2, fields, rows),
            held(fields, rows),
            held(fields, rows),
            held(fields, rows),
            held(fields, own),
            held(fields, own),
            held(fields, own),
            held(2, fields, own),
            held(fields, own),
            dma((5, strips)),
            dma((4,)),
            dma((2,)),
            dma((moments - 1,)),
            dma((moments - 1,)),
            dma((rows // lift_piece,)),
            dma((rows // lift_piece,)),
            dma((chunks,)),
            dma((chunks,)),
            dma((chunks,)),
            dma((chunks,)),
            dma((chunks,)),
            dma((chunks,)),
            dma((chunks,)),
            dma((chunks,)),
            dma((chunks,)),
            dma((2,)),
            dma((2,)),
            dma((2,)),
            dma((2,)),
            dma((2,)),
            dma((3,)),
            dma((3,)),
            pltpu.SemaphoreType.REGULAR,
        ],
        compiler_params=pltpu.CompilerParams(
            collective_id=0, has_side_effects=True, vmem_limit_bytes=32 * 1024 * 1024
        ),
    )(*(
        pltpu.with_memory_space_constraint(array, pltpu.HBM)
        for array in (cpoint_guess, tide_forcing, depth, drag)
    ))
    return pl.pallas_call(
        finish_kernel,
        out_shape=(
            jax.ShapeDtypeStruct(tide_forcing.shape, jnp.float32),
            jax.ShapeDtypeStruct(cpoint_guess.shape, jnp.float32),
        ),
        in_specs=[vmem] * 5,
        out_specs=(hbm, hbm),
        scratch_shapes=[
            held(2, fields, rows),
            held(fields, rows),
            held(moments, fields, own),
            held(fields, own),
            dma((moments + 1, strips)),
        ],
        compiler_params=pltpu.CompilerParams(vmem_limit_bytes=16 * 1024 * 1024),
    )(*passed_on)


def solution(mesh):
    placed = (
        P("tm", None, "space", None),
        P("tm", None, "space", None),
        P("space", None),
        P("space", None),
    )
    one_top_point = mesh.shape["tm"] == 2 ** (LEVELS - 1)
    fits = one_top_point and mesh.shape["space"] == 2
    return jax.shard_map(
        kernel_body if fits else body,
        mesh=mesh,
        in_specs=placed,
        out_specs=(P("tm", None, "space", None), P("tm", None, "space", None)),
        check_vma=False,
    )
```
